128 devices in a mesh: seq: 64 (over y, z, x), dp: 2 (over core).
Axes of the slice: x: 4, y: 4, z: 4, core: 2. Of those that a mesh axis runs over, the one named last changes fastest.
Arguments:
- queries: bfloat16 [131072, 768], P(('dp', 'seq')), parts along dimension 0, may hold values from -2.5 to 2.5
- keys: bfloat16 [131072, 768], P(('dp', 'seq')), parts along dimension 0, may hold values from -2.5 to 2.5
- values: bfloat16 [131072, 768], P(('dp', 'seq')), parts along dimension 0, may hold values from -6 to 6
- norm_gain: float32 [768], replicated, may hold values from 0.5 to 1.5
- expert_ids: int32 [131072, 1], P(('dp', 'seq')), parts along dimension 0, may hold values from 0 to 127; in each aligned block of 1024 rows (0 to 1023, 1024 to 2047, ...) at most 12 rows name the same one
- w_in: bfloat16 [256, 768, 3072], P(('dp', 'seq')), parts along dimension 0, may hold values from -0.21875 to 0.21875
- w_out: bfloat16 [256, 3072, 768], P(('dp', 'seq')), parts along dimension 0, may hold values from -0.109375 to 0.109375
Outputs:
- block_output: bfloat16 [131072, 768], P(('dp', 'seq')), parts along dimension 0
The draws below stay inside these ranges and needn't reach their ends.
There are 2 independent parts, one for each index of `dp`. The reference program is written for one: setup_inputs(seed, part) draws one part's arguments, and reference() takes and returns one part's arrays. A program takes and returns all parts, laid end to end along the dimension named above; an argument that names none is the same for every part. Nothing has to cross between parts.
Inputs may be any that keep to these rules, and one draw needn't show every extreme that they name: `expert_ids`: within each aligned block of 1024 rows no expert is named more than 12 times, and in every draw some expert is named exactly 12 times in some block.
All inputs are finite; a program needn't handle non-finite values.
Results may differ from the reference program's by a relative error of at most 0.008.
Values may be sent and summed in bfloat16 or wider, within the bound.
A program may use at most 128 MiB of HBM per device.

```python
import math
import jax
import jax.numpy as jnp
import numpy as np
from jax import lax

HEADS = 12
D = 768
FF = 3072
EXPERTS = 128
TOK_DEV = 1024
TOKENS = 65536
CAP = 12
N_SEQ = 64


def block_levels(rng, extent, cuts, smallest, largest):
    gain, own = 1.0, jax.random.fold_in(rng, 6)
    for position, blocks in cuts:
        draws = jnp.exp(jax.random.uniform(jax.random.fold_in(own, position), (blocks,), jnp.float32, smallest / len(cuts), largest / len(cuts)))
        gain = gain * jnp.repeat(draws, extent[position] // blocks).reshape([-1 if axis == position else 1 for axis in range(len(extent))])
    return gain


def routed_block(key, own, number, rows, number_of, top, bound, slope):
    sequence = jax.random.permutation(key, number_of)
    crowded, usual = load_shares(number_of, rows * top, bound, slope, True), load_shares(number_of, rows * top, bound, slope, False)
    places = jnp.arange(number_of)

    def named(sizes, offset_by):
        used = int((sizes > 0).sum())
        fixed = max(1, used // 4)
        passed = fixed + (places - fixed + offset_by * (used - fixed)) % max(1, number_of - fixed)
        return jnp.zeros((number_of,), jnp.int32).at[sequence[jnp.where(places < fixed, places, passed)]].set(jnp.asarray(sizes, jnp.int32))

    sizes = jnp.where(number % 4 == 0, named(crowded, number // 4), named(usual, number - number // 4 - 1))
    mixed = jax.random.permutation(jax.random.fold_in(own, 3), number_of)
    giver, receiver = mixed[0:number_of // 2 * 2:2], mixed[1:number_of // 2 * 2:2]
    margin = jnp.minimum(sizes[giver] - 1, bound - sizes[receiver]) // 2
    margin = jnp.where((giver == sequence[0]) | (receiver == sequence[0]) | (sizes[receiver] == 0), 0, jnp.maximum(margin, 0))
    passed = jax.random.randint(jax.random.fold_in(own, 4), (number_of // 2,), 0, 1 << 20) % (margin + 1)
    sizes = sizes.at[giver].add(-passed).at[receiver].add(passed)
    labels = jnp.searchsorted(jnp.cumsum(sizes), jnp.arange(rows * top), side="right").astype(jnp.int32)
    grid = labels.reshape(top, rows).T
    grid = grid[jax.random.permutation(jax.random.fold_in(own, 1), rows)]
    offset_by = jax.random.randint(jax.random.fold_in(own, 2), (rows, 1), 0, top)
    return jnp.take_along_axis(grid, (jnp.arange(top)[None, :] + offset_by) % top, axis=1)


def load_shares(count, total, most, lean, full):
    portions = [(1 << 20) // math.isqrt(standing ** lean) + 1 for standing in range(1, count + 1)]
    largest = most if full else min(most, max(-(-total // count), total * portions[0] // sum(portions)))
    least = 1 if total - largest >= count - 1 else 0
    given, surplus = [largest] + [least] * (count - 1), total - largest - least * (count - 1)
    while surplus > 0:
        candidates = [i for i in range(1, count) if given[i] < largest] or [i for i in range(1, count) if given[i] < most]
        mass, budget = sum([portions[i] for i in candidates]), surplus
        for i in candidates:
            addition = min(most - given[i], max(1, budget * portions[i] // mass), surplus)
            given[i] = given[i] + addition
            surplus = surplus - addition
    return np.array(given)


def gaussian(own_key, shape, width, most, cuts=(), kind=jnp.bfloat16):
    result = width * jax.random.normal(own_key, shape, jnp.float32)
    if cuts:
        result = result * block_levels(own_key, shape, cuts, -0.22, 0.18)
    return jnp.clip(result, -most, most).astype(kind)


def setup_inputs(seed: int = 0, part: int = 0) -> dict:
    streams_of = jax.random.split(jax.random.key(seed), 8)
    part_keys = jax.random.split(jax.random.fold_in(streams_of[7], part), 8)
    queries = gaussian(part_keys[0], (TOKENS, D), 0.35, 2.5, ((0, 64),))
    keys = gaussian(part_keys[1], (TOKENS, D), 0.35, 2.5, ((0, 64),))
    values = gaussian(part_keys[2], (TOKENS, D), 1.0, 6.0, ((0, 64),))
    norm_gain = jnp.clip(1.0 + 0.1 * jax.random.normal(streams_of[3], (D,), jnp.float32), 0.5, 1.5)
    expert_ids_keys = jax.random.split(jax.random.fold_in(part_keys[4], 1), TOKENS // TOK_DEV)
    expert_ids_turns = jax.random.permutation(jax.random.fold_in(part_keys[4], 3), TOKENS // TOK_DEV)
    expert_ids = jax.vmap(lambda own, number: routed_block(jax.random.fold_in(part_keys[4], 2), own, number, TOK_DEV, EXPERTS, 1, CAP, 2))(expert_ids_keys, expert_ids_turns).reshape((TOKENS, 1))
    w_in = gaussian(part_keys[5], (EXPERTS, D, FF), D ** -0.5, 0.21875, ((0, 64),))
    w_out = gaussian(part_keys[6], (EXPERTS, FF, D), FF ** -0.5, 0.109375, ((0, 64),))
    return {"queries": queries, "keys": keys, "values": values, "norm_gain": norm_gain, "expert_ids": expert_ids, "w_in": w_in, "w_out": w_out}


epsilon = 1e-06

def attend(queries, keys, values):
    head_width = D // HEADS
    query_blocks = queries.reshape(N_SEQ, TOK_DEV, HEADS, head_width)
    key_blocks = keys.reshape(N_SEQ, TOK_DEV, HEADS, head_width)
    value_blocks = values.reshape(N_SEQ, TOK_DEV, HEADS, head_width)
    causal = jnp.arange(TOK_DEV)[:, None] >= jnp.arange(TOK_DEV)[None, :]

    def one_block(carried, blocks):
        query_heads, key_heads, value_heads = blocks
        scores = jnp.einsum('thd,shd->hts', query_heads.astype(jnp.float32), key_heads.astype(jnp.float32))
        scores = jnp.where(causal[None], scores, 0.0).astype(jnp.bfloat16)
        local_part = jnp.einsum('hts,shd->thd', scores.astype(jnp.float32), value_heads.astype(jnp.float32))
        carried_part = jnp.einsum('thd,hde->the', query_heads.astype(jnp.float32), carried, precision=lax.Precision.HIGHEST)
        block_state = jnp.einsum('thd,the->hde', key_heads.astype(jnp.float32), value_heads.astype(jnp.float32))
        return (carried + block_state, local_part + carried_part)
    start_state = jnp.zeros((HEADS, head_width, head_width), jnp.float32)
    final_state, mixed = lax.scan(one_block, start_state, (query_blocks, key_blocks, value_blocks))
    return mixed.reshape(TOKENS, D)

def reference(queries, keys, values, norm_gain, expert_ids, w_in, w_out):
    mixed = attend(queries, keys, values)
    scale = lax.rsqrt(lax.optimization_barrier(jnp.mean(mixed * mixed, axis=-1, keepdims=True)) + epsilon)
    normed = (mixed * scale * norm_gain).astype(jnp.bfloat16)
    routes = expert_ids[:, 0].astype(jnp.int32)
    sort_order = jnp.argsort(routes, stable=True).astype(jnp.int32)
    expert_counts = jnp.zeros((EXPERTS,), jnp.int32).at[routes].add(1)
    expert_starts = (jnp.cumsum(expert_counts) - expert_counts).astype(jnp.int32)
    window = N_SEQ * CAP
    padded_rows = jnp.concatenate([normed[sort_order], jnp.zeros((window, D), jnp.bfloat16)], axis=0)

    def run_expert(expert_index):
        window_rows = lax.dynamic_slice(padded_rows, (expert_starts[expert_index], jnp.int32(0)), (window, D))
        hidden = jnp.dot(window_rows, w_in[expert_index], preferred_element_type=jnp.float32)
        hidden = jnp.maximum(hidden, 0.0).astype(jnp.bfloat16)
        return jnp.dot(hidden, w_out[expert_index], preferred_element_type=jnp.float32).astype(jnp.bfloat16)
    expert_rows = lax.map(run_expert, jnp.arange(EXPERTS, dtype=jnp.int32))
    sorted_routes = routes[sort_order]
    slot_rank = (jnp.arange(TOKENS, dtype=jnp.int32) - expert_starts[sorted_routes]).astype(jnp.int32)
    sorted_out = expert_rows[sorted_routes, slot_rank]
    expert_out = jnp.zeros((TOKENS, D), jnp.bfloat16).at[sort_order].set(sorted_out)
    return (normed.astype(jnp.float32) + expert_out.astype(jnp.float32)).astype(jnp.bfloat16)
```

```python
import jax
import jax.numpy as jnp
from jax import lax
from jax.experimental import pallas as pl
from jax.experimental.pallas import tpu as pltpu
from jax.sharding import PartitionSpec as P

MESH = pl.DeviceIdType.MESH
EPS = 1e-06
F32 = jnp.float32
BF16 = jnp.bfloat16

N = 64
T = 1024
D = 768
FF = 3072
E = 128
PAIRS = 6
C = 256
NC = T // C
OWN = 48
CH = 3
M = 512


def dot(a, b):
    return jnp.dot(a, b, preferred_element_type=F32)


def dot_nt(a, b):
    return lax.dot_general(a, b, (((1,), (1,)), ((), ())), preferred_element_type=F32)


def dot_tn(a, b):
    return lax.dot_general(a, b, (((0,), (0,)), ((), ())), preferred_element_type=F32)


def lanes(p, width=128):
    return pl.ds(pl.multiple_of(p * width, width), width)


def body(q_hbm, k_hbm, v_hbm, gain_ref, ids_ref, win_hbm, wout_hbm, out_ref,
         q_ref, k_ref, v_ref, win, wout, kv_ref, cst_ref, mixed_ref, normed_ref,
         st_send, st_recv, pre_send, pre_recv, slot_ref, disp_send, disp_recv, ret_send, ret_recv,
         a_ref, h_ref, acc_ref,
         ld_sem, w_sem, self_sem, st_sem, pre_sem, disp_ssem, disp_rsem, ret_ssem, ret_rsem):
    me = lax.axis_index("seq")

    def remote(src, dst, ssem, rsem, d):
        return pltpu.make_async_remote_copy(
            src_ref=src, dst_ref=dst, send_sem=ssem, recv_sem=rsem,
            device_id={"seq": d}, device_id_type=MESH)

    barrier = pltpu.get_barrier_semaphore()

    def greet(o, _):
        pl.semaphore_signal(barrier, inc=1, device_id={"seq": lax.rem(me + o, N)}, device_id_type=MESH)
        return 0
    lax.fori_loop(1, N, greet, 0)

    loads = [pltpu.make_async_copy(s, d, ld_sem.at[i])
             for i, (s, d) in enumerate(((k_hbm, k_ref), (v_hbm, v_ref), (q_hbm, q_ref)))]
    for c in loads:
        c.start()
    weights = [pltpu.make_async_copy(s.at[e], d.at[e], w_sem.at[2 * e + i])
               for e in range(2) for i, (s, d) in enumerate(((win_hbm, win), (wout_hbm, wout)))]
    for c in weights:
        c.start()

    lane = lax.broadcasted_iota(jnp.int32, (1, 128), 1)
    low = lane < 64

    loads[0].wait()
    loads[1].wait()
    row128 = lax.broadcasted_iota(jnp.int32, (128, 128), 0)
    lane128 = lax.broadcasted_iota(jnp.int32, (128, 128), 1)
    diag = (row128 < 64) == (lane128 < 64)

    def states(p, _):
        total = jnp.zeros((128, 128), F32)
        for c in range(NC):
            kv_ref[p, c] = total
            kc = k_ref[c * C:(c + 1) * C, lanes(p)]
            vc = v_ref[c * C:(c + 1) * C, lanes(p)]
            total = total + jnp.where(diag, dot_tn(kc, vc), 0.0)
        compact = jnp.where(low, total[:64], total[64:])
        st_send[pl.ds(p * 8, 8)] = compact.reshape(8, 8, 128).astype(BF16)
        return 0
    lax.fori_loop(0, PAIRS, states, 0)

    pl.semaphore_wait(barrier, N - 1)

    def send_state(d, _):
        @pl.when(d != me)
        def _():
            remote(st_send.at[d], st_recv.at[me], st_sem.at[0], st_sem.at[1], d).start()
        return 0
    lax.fori_loop(0, OWN, send_state, 0)

    @pl.when(me < OWN)
    def _():
        pltpu.make_async_copy(st_send.at[me], st_recv.at[me], self_sem.at[0]).start()

    loads[2].wait()
    tri = lax.broadcasted_iota(jnp.int32, (C, C), 0) >= lax.broadcasted_iota(jnp.int32, (C, C), 1)

    def local(p, _):
        for c in range(NC):
            rows = slice(c * C, (c + 1) * C)
            qc = q_ref[rows, lanes(p)]
            kc = k_ref[rows, lanes(p)]
            vc = v_ref[rows, lanes(p)]
            zero = jnp.zeros_like(kc)
            s0 = jnp.where(tri, dot_nt(qc, jnp.where(low, kc, zero)), 0.0).astype(BF16)
            s1 = jnp.where(tri, dot_nt(qc, jnp.where(low, zero, kc)), 0.0).astype(BF16)
            mixed_ref[rows, lanes(p)] = dot(s0, jnp.where(low, vc, zero)) + dot(s1, jnp.where(low, zero, vc))
        return 0
    lax.fori_loop(0, 4, local, 0)

    @pl.when(me < OWN)
    def _():
        pltpu.make_async_copy(st_send.at[me], st_recv.at[me], self_sem.at[0]).wait()
        pltpu.make_async_copy(st_recv.at[pl.ds(0, N - 1)], st_recv.at[pl.ds(0, N - 1)], st_sem.at[1]).wait()

        def step(i, run):
            pre_send[i] = run.astype(BF16)
            return run + st_recv[i].astype(F32)
        lax.fori_loop(0, N, step, jnp.zeros((8, 128), F32), unroll=8)

        def send_prefix(o, _):
            d = lax.rem(me + o, N)
            remote(pre_send.at[d], pre_recv.at[me], pre_sem.at[0], pre_sem.at[1], d).start()
            return 0
        lax.fori_loop(1, N, send_prefix, 0)
        pltpu.make_async_copy(pre_send.at[me], pre_recv.at[me], self_sem.at[1]).start()

    lax.fori_loop(4, PAIRS, local, 0)

    ids = ids_ref[...]
    trib = jnp.where(lax.broadcasted_iota(jnp.int32, (C, C), 0) <= lax.broadcasted_iota(jnp.int32, (C, C), 1),
                     1.0, 0.0).astype(BF16)
    expert = lax.broadcasted_iota(jnp.int32, (E, C), 0)
    before = jnp.zeros((E, 1), F32)
    pieces = []
    for c in range(NC):
        idc = ids[:, c * C:(c + 1) * C]
        match = jnp.where(expert == idc, 1.0, 0.0)
        running = dot(match.astype(BF16), trib) + before
        rank = jnp.sum(running * match, axis=0, keepdims=True).astype(jnp.int32) - 1
        before = before + jnp.sum(match, axis=1, keepdims=True)
        half = lax.rem(idc, 2)
        owner = lax.div(idc, 2)
        pieces.append(jnp.where(rank < 8, half * M + owner * 8 + rank, 2 * M + owner * 8 + half * 4 + rank - 8))
    slot_row = jnp.concatenate(pieces, axis=1)
    slot_ref[...] = jnp.transpose(jnp.broadcast_to(slot_row.astype(F32), (128, T))).astype(jnp.int32)

    @pl.when(me < OWN)
    def _():
        pltpu.make_async_copy(pre_send.at[me], pre_recv.at[me], self_sem.at[1]).wait()
        pltpu.make_async_copy(pre_recv.at[pl.ds(0, OWN - 1)], pre_recv.at[pl.ds(0, OWN - 1)], pre_sem.at[1]).wait()

    @pl.when(me >= OWN)
    def _():
        pltpu.make_async_copy(pre_recv, pre_recv, pre_sem.at[1]).wait()

    for p in range(PAIRS):
        compact = pre_recv[pl.ds(p * 8, 8)].astype(F32).reshape(64, 128)
        cst_ref[p, :64] = jnp.where(low, compact, 0.0)
        cst_ref[p, 64:] = jnp.where(low, 0.0, compact)

    def finish(c, _):
        rows = pl.ds(pl.multiple_of(c * C, C), C)
        square = jnp.zeros((C, 128), F32)
        for p in range(PAIRS):
            cols = slice(p * 128, (p + 1) * 128)
            state = (kv_ref[p, c] + cst_ref[p]).astype(BF16)
            m = mixed_ref[rows, cols] + dot(q_ref[rows, cols], state)
            mixed_ref[rows, cols] = m
            square = square + m * m
        scale = lax.rsqrt(jnp.sum(square, axis=1, keepdims=True) * (1.0 / D) + EPS)
        normed_ref[rows, :] = (mixed_ref[rows, :] * scale * gain_ref[...]).astype(BF16)
        return 0
    lax.fori_loop(0, NC, finish, 0)

    for ch in range(CH):
        pick = jnp.where(lax.broadcasted_iota(jnp.int32, (M, T), 0) == slot_row - ch * M, 1.0, 0.0).astype(BF16)
        for n in range(3):
            y = dot(pick, normed_ref[:, n * 256:(n + 1) * 256])
            disp_send[ch, :, 2 * n] = y[:, :128].reshape(N, 8, 128).astype(BF16)
            disp_send[ch, :, 2 * n + 1] = y[:, 128:].reshape(N, 8, 128).astype(BF16)

        def send_rows(o, _):
            d = lax.rem(me + o * 21, N)
            remote(disp_send.at[ch, d], disp_recv.at[ch, me], disp_ssem.at[ch], disp_rsem.at[ch], d).start()
            return 0
        lax.fori_loop(1, N, send_rows, 0)
        pltpu.make_async_copy(disp_send.at[ch, me], disp_recv.at[ch, me], self_sem.at[2 + ch]).start()

    top = lax.broadcasted_iota(jnp.int32, (1, 8, 128), 1) < 4

    def ffn(e, start, rows, put):
        def first(f, _):
            hid = dot(a_ref[start:start + rows, :], win[e, :, lanes(f, 256)])
            h_ref[start:start + rows, lanes(f, 256)] = jnp.maximum(hid, 0.0).astype(BF16)
            return 0
        lax.fori_loop(0, FF // 256, first, 0)

        def second(n, _):
            put(n, dot(h_ref[start:start + rows, :], wout[e, :, lanes(n, 256)]))
            return 0
        lax.fori_loop(0, D // 256, second, 0)

    def bulk(buf, sem):
        return pltpu.make_async_copy(buf.at[pl.ds(0, N - 1)], buf.at[pl.ds(0, N - 1)], sem)

    for ch in range(CH):
        pltpu.make_async_copy(disp_send.at[ch, me], disp_recv.at[ch, me], self_sem.at[2 + ch]).wait()
        bulk(disp_recv.at[ch], disp_rsem.at[ch]).wait()
        if ch < 2:
            weights[2 * ch].wait()
            weights[2 * ch + 1].wait()
            for j in range(6):
                a_ref[:, j * 128:(j + 1) * 128] = disp_recv[ch, :, j].astype(F32).reshape(M, 128).astype(BF16)

            def put(n, o):
                ret_send[ch, :, 2 * n] = o[:, :128].reshape(N, 8, 128).astype(BF16)
                ret_send[ch, :, 2 * n + 1] = o[:, 128:].reshape(N, 8, 128).astype(BF16)
            ffn(ch, 0, M, put)
        else:
            for j in range(6):
                x = disp_recv[ch, :, j].astype(F32).reshape(N // 2, 2, 8, 128)
                even, odd = x[:, 0], x[:, 1]
                x0 = jnp.where(top, even, pltpu.roll(odd, 4, 1))
                x1 = jnp.where(top, pltpu.roll(even, 4, 1), odd)
                a_ref[:256, j * 128:(j + 1) * 128] = x0.reshape(256, 128).astype(BF16)
                a_ref[256:, j * 128:(j + 1) * 128] = x1.reshape(256, 128).astype(BF16)

            def put0(n, o):
                acc_ref[:256, lanes(n, 256)] = o

            def put1(n, o):
                acc_ref[256:512, lanes(n, 256)] = o
            ffn(0, 0, 256, put0)
            ffn(1, 256, 256, put1)
            for j in range(6):
                o0 = acc_ref[:256, j * 128:(j + 1) * 128].reshape(N // 2, 8, 128)
                o1 = acc_ref[256:512, j * 128:(j + 1) * 128].reshape(N // 2, 8, 128)
                even = jnp.where(top, o0, pltpu.roll(o1, 4, 1))
                odd = jnp.where(top, pltpu.roll(o0, 4, 1), o1)
                ret_send[ch, :, j] = jnp.stack([even, odd], axis=1).reshape(N, 8, 128).astype(BF16)

        def send_back(o, _):
            d = lax.rem(me + o * 21, N)
            remote(ret_send.at[ch, d], ret_recv.at[ch, me], ret_ssem.at[ch], ret_rsem.at[ch], d).start()
            return 0
        lax.fori_loop(1, N, send_back, 0)
        pltpu.make_async_copy(ret_send.at[ch, me], ret_recv.at[ch, me], self_sem.at[5 + ch]).start()

    for ch in range(CH):
        pltpu.make_async_copy(ret_send.at[ch, me], ret_recv.at[ch, me], self_sem.at[5 + ch]).wait()
        bulk(ret_recv.at[ch], ret_rsem.at[ch]).wait()
        for j in range(6):
            a_ref[:, j * 128:(j + 1) * 128] = ret_recv[ch, :, j].astype(F32).reshape(M, 128).astype(BF16)

        def unpack(c, _):
            rows = pl.ds(pl.multiple_of(c * C, C), C)
            place = slot_ref[rows, :] - ch * M
            back = jnp.concatenate([jnp.where(place == lane + 128 * i, 1.0, 0.0).astype(BF16) for i in range(M // 128)], axis=1)
            for n in range(3):
                cols = slice(n * 256, (n + 1) * 256)
                y = dot(back, a_ref[:, cols])
                if ch == 0:
                    acc_ref[rows, cols] = y
                elif ch == 1:
                    acc_ref[rows, cols] = acc_ref[rows, cols] + y
                else:
                    total = acc_ref[rows, cols] + y
                    out_ref[rows, cols] = (normed_ref[rows, cols].astype(F32) + total).astype(BF16)
            return 0
        lax.fori_loop(0, NC, unpack, 0)

    @pl.when(me < OWN)
    def _():
        pltpu.make_async_copy(st_send.at[pl.ds(0, OWN - 1)], st_send.at[pl.ds(0, OWN - 1)], st_sem.at[0]).wait()
        bulk(pre_send, pre_sem.at[0]).wait()

    @pl.when(me >= OWN)
    def _():
        pltpu.make_async_copy(st_send, st_send, st_sem.at[0]).wait()
    for ch in range(CH):
        bulk(disp_send.at[ch], disp_ssem.at[ch]).wait()
        bulk(ret_send.at[ch], ret_ssem.at[ch]).wait()


def shards(queries, keys, values, norm_gain, expert_ids, w_in, w_out):
    hbm = pl.BlockSpec(memory_space=pl.ANY)
    vmem = pl.BlockSpec(memory_space=pltpu.VMEM)
    dma = pltpu.SemaphoreType.DMA
    return pl.pallas_call(
        body,
        out_shape=jax.ShapeDtypeStruct((T, D), BF16),
        in_specs=[hbm, hbm, hbm, vmem, vmem, hbm, hbm],
        out_specs=vmem,
        scratch_shapes=[
            pltpu.VMEM((T, D), BF16), pltpu.VMEM((T, D), BF16), pltpu.VMEM((T, D), BF16),
            pltpu.VMEM((2, D, FF), BF16), pltpu.VMEM((2, FF, D), BF16),
            pltpu.VMEM((PAIRS, NC, 128, 128), F32), pltpu.VMEM((PAIRS, 128, 128), F32),
            pltpu.VMEM((T, D), F32), pltpu.VMEM((T, D), BF16),
            pltpu.VMEM((OWN, 8, 128), BF16), pltpu.VMEM((N, 8, 128), BF16),
            pltpu.VMEM((N, 8, 128), BF16), pltpu.VMEM((OWN, 8, 128), BF16),
            pltpu.VMEM((T, 128), jnp.int32),
            pltpu.VMEM((CH, N, 6, 8, 128), BF16), pltpu.VMEM((CH, N, 6, 8, 128), BF16),
            pltpu.VMEM((CH, N, 6, 8, 128), BF16), pltpu.VMEM((CH, N, 6, 8, 128), BF16),
            pltpu.VMEM((M, D), BF16), pltpu.VMEM((M, FF), BF16), pltpu.VMEM((T, D), F32),
            dma((3,)), dma((4,)), dma((8,)), dma((2,)), dma((2,)),
            dma((CH,)), dma((CH,)), dma((CH,)), dma((CH,)),
        ],
        compiler_params=pltpu.CompilerParams(
            collective_id=0, has_side_effects=True, vmem_limit_bytes=67043328),
        name="block",
    )(queries, keys, values, norm_gain.reshape(1, D), expert_ids.reshape(1, T), w_in, w_out)


def solution(mesh):
    rows = P(("dp", "seq"), None)
    weights = P(("dp", "seq"), None, None)
    return jax.shard_map(
        shards, mesh=mesh, in_specs=(rows, rows, rows, P(), rows, weights, weights),
        out_specs=rows, check_vma=False)
```

```python
import jax
import jax.numpy as jnp
from jax import lax
from jax.experimental import pallas as pl
from jax.experimental.pallas import tpu as pltpu
from jax.sharding import PartitionSpec as P

MESH = pl.DeviceIdType.MESH
EPS = 1e-06
F32 = jnp.float32
BF16 = jnp.bfloat16

N = 64
T = 1024
D = 768
FF = 3072
E = 128
PAIRS = 6
C = 256
NC = T // C
OWN = 48
CH = 3
M = 512


def hops(o):
    return sum((0, 1, 2, 1)[g] for g in (o // 16, o // 4 % 4, o % 4))


ORDER = sorted(range(1, N), key=lambda o: (-hops(o), o * 37 % 64))
MIXED = [o * 21 % 64 for o in range(1, N)]


def dot(a, b):
    return jnp.dot(a, b, preferred_element_type=F32)


def dot_nt(a, b):
    return lax.dot_general(a, b, (((1,), (1,)), ((), ())), preferred_element_type=F32)


def dot_tn(a, b):
    return lax.dot_general(a, b, (((0,), (0,)), ((), ())), preferred_element_type=F32)


def lanes(p, width=128):
    return pl.ds(pl.multiple_of(p * width, width), width)


def spread(place):
    lane = lax.broadcasted_iota(jnp.int32, (1, 128), 1)
    return jnp.concatenate([jnp.where(place == lane + 128 * i, 1.0, 0.0).astype(BF16) for i in range(M // 128)], axis=1)


def body(q_hbm, k_hbm, v_hbm, gain_hbm, ids_hbm, win_hbm, wout_hbm,
         out_ref,
         gain_ref, ids_ref, q_ref, k_ref, v_ref, win, wout, kv_ref, cst_ref, mixed_ref, normed_ref,
         st_send, st_recv, pre_send, pre_recv, slot_ref, early_ref, earlyq_ref, disp_send, disp_recv, ret_send, ret_recv,
         a_ref, h_ref, acc_ref,
         ld_sem, w_sem, self_sem, st_sem, pre_sem, disp_ssem, disp_rsem, ret_ssem, ret_rsem):
    me = lax.axis_index("seq")
    my, mz, mx = me // 16, lax.rem(me // 4, 4), lax.rem(me, 4)
    ys = [lax.rem(my + g, 4) * 16 for g in range(4)]
    zs = [lax.rem(mz + g, 4) * 4 for g in range(4)]
    xs = [lax.rem(mx + g, 4) for g in range(4)]

    def other(o):
        return ys[o // 16] + zs[o // 4 % 4] + xs[o % 4]

    def remote(src, dst, ssem, rsem, d):
        return pltpu.make_async_remote_copy(
            src_ref=src, dst_ref=dst, send_sem=ssem, recv_sem=rsem,
            device_id={"seq": d}, device_id_type=MESH)

    barrier = pltpu.get_barrier_semaphore()

    for o in ORDER:
        pl.semaphore_signal(barrier, inc=1, device_id={"seq": other(o)}, device_id_type=MESH)

    loads = [pltpu.make_async_copy(s, d, ld_sem.at[i])
             for i, (s, d) in enumerate(((k_hbm, k_ref), (v_hbm, v_ref), (ids_hbm, ids_ref), (gain_hbm, gain_ref), (q_hbm, q_ref)))]
    for c in loads:
        c.start()
    weights = [pltpu.make_async_copy(s.at[e], d.at[e], w_sem.at[2 * e + i])
               for e in range(2) for i, (s, d) in enumerate(((win_hbm, win), (wout_hbm, wout)))]
    for c in weights:
        c.start()

    lane = lax.broadcasted_iota(jnp.int32, (1, 128), 1)
    low = lane < 64

    loads[0].wait()
    loads[1].wait()
    row128 = lax.broadcasted_iota(jnp.int32, (128, 128), 0)
    lane128 = lax.broadcasted_iota(jnp.int32, (128, 128), 1)
    diag = (row128 < 64) == (lane128 < 64)

    def states(p, _):
        total = jnp.zeros((128, 128), F32)
        for c in range(NC):
            kv_ref[p, c] = total
            kc = k_ref[c * C:(c + 1) * C, lanes(p)]
            vc = v_ref[c * C:(c + 1) * C, lanes(p)]
            total = total + jnp.where(diag, dot_tn(kc, vc), 0.0)
        compact = jnp.where(low, total[:64], total[64:])
        st_send[pl.ds(p * 8, 8)] = compact.reshape(8, 8, 128).astype(BF16)
        return 0
    lax.fori_loop(0, PAIRS, states, 0)

    loads[2].wait()
    loads[3].wait()
    ids = ids_ref[...]
    trib = jnp.where(lax.broadcasted_iota(jnp.int32, (C, C), 0) <= lax.broadcasted_iota(jnp.int32, (C, C), 1),
                     1.0, 0.0).astype(BF16)
    expert = lax.broadcasted_iota(jnp.int32, (E, C), 0)
    before = jnp.zeros((E, 1), F32)
    pieces = []
    for c in range(NC):
        idc = ids[:, c * C:(c + 1) * C]
        match = jnp.where(expert == idc, 1.0, 0.0)
        running = dot(match.astype(BF16), trib) + before
        rank = jnp.sum(running * match, axis=0, keepdims=True).astype(jnp.int32) - 1
        before = before + jnp.sum(match, axis=1, keepdims=True)
        half = lax.rem(idc, 2)
        owner = lax.div(idc, 2)
        pieces.append(jnp.where(rank < 8, half * M + owner * 8 + rank, 2 * M + owner * 8 + half * 4 + rank - 8))
    slot_row = jnp.concatenate(pieces, axis=1)
    slot_ref[...] = jnp.transpose(jnp.broadcast_to(slot_row.astype(F32), (128, T))).astype(jnp.int32)

    pl.semaphore_wait(barrier, N - 1)
    for o in ORDER:
        d = other(o)

        @pl.when(d < OWN)
        def _(d=d):
            remote(st_send.at[d], st_recv.at[me], st_sem.at[0], st_sem.at[1], d).start()

    @pl.when(me < OWN)
    def _():
        pltpu.make_async_copy(st_send.at[me], st_recv.at[me], self_sem.at[0]).start()

    loads[4].wait()
    tri = lax.broadcasted_iota(jnp.int32, (C, C), 0) >= lax.broadcasted_iota(jnp.int32, (C, C), 1)

    def local(p, _):
        for c in range(NC):
            rows = slice(c * C, (c + 1) * C)
            qc = q_ref[rows, lanes(p)]
            kc = k_ref[rows, lanes(p)]
            vc = v_ref[rows, lanes(p)]
            zero = jnp.zeros_like(kc)
            s0 = jnp.where(tri, dot_nt(qc, jnp.where(low, kc, zero)), 0.0).astype(BF16)
            s1 = jnp.where(tri, dot_nt(qc, jnp.where(low, zero, kc)), 0.0).astype(BF16)
            mixed_ref[rows, lanes(p)] = (dot(s0, jnp.where(low, vc, zero)) + dot(s1, jnp.where(low, zero, vc))
                                         + dot(qc, kv_ref[p, c].astype(BF16)))
        return 0
    lax.fori_loop(0, PAIRS, local, 0)

    @pl.when(me < OWN)
    def _():
        pltpu.make_async_copy(st_send.at[me], st_recv.at[me], self_sem.at[0]).wait()
        pltpu.make_async_copy(st_recv.at[pl.ds(0, N - 1)], st_recv.at[pl.ds(0, N - 1)], st_sem.at[1]).wait()

        def step(i, run):
            pre_send[i] = run.astype(BF16)
            return run + st_recv[i].astype(F32)
        lax.fori_loop(0, N, step, jnp.zeros((8, 128), F32), unroll=8)

        for o in ORDER:
            d = other(o)
            remote(pre_send.at[d], pre_recv.at[me], pre_sem.at[0], pre_sem.at[1], d).start()
        pltpu.make_async_copy(pre_send.at[me], pre_recv.at[me], self_sem.at[1]).start()

    def pick(ch):
        return jnp.where(lax.broadcasted_iota(jnp.int32, (M, T), 0) == slot_row - ch * M, 1.0, 0.0).astype(BF16)

    first_pick = pick(0)
    for n in range(3):
        cols = slice(n * 256, (n + 1) * 256)
        m = mixed_ref[:, cols]
        high = m.astype(BF16)
        early_ref[:, cols] = dot(first_pick, high) + dot(first_pick, (m - high.astype(F32)).astype(BF16))
        earlyq_ref[:, cols] = dot(first_pick, q_ref[:, cols]).astype(BF16)

    @pl.when(me < OWN)
    def _():
        pltpu.make_async_copy(pre_send.at[me], pre_recv.at[me], self_sem.at[1]).wait()
        pltpu.make_async_copy(pre_recv.at[pl.ds(0, OWN - 1)], pre_recv.at[pl.ds(0, OWN - 1)], pre_sem.at[1]).wait()

    @pl.when(me >= OWN)
    def _():
        pltpu.make_async_copy(pre_recv, pre_recv, pre_sem.at[1]).wait()

    for p in range(PAIRS):
        compact = pre_recv[pl.ds(p * 8, 8)].astype(F32).reshape(64, 128)
        cst_ref[p, :64] = jnp.where(low, compact, 0.0).astype(BF16)
        cst_ref[p, 64:] = jnp.where(low, 0.0, compact).astype(BF16)

    gain = gain_ref[...].reshape(1, D)

    def send_rows(ch):
        for o in MIXED:
            d = other(o)
            remote(disp_send.at[ch, d], disp_recv.at[ch, me], disp_ssem.at[ch], disp_rsem.at[ch], d).start()
        pltpu.make_async_copy(disp_send.at[ch, me], disp_recv.at[ch, me], self_sem.at[2 + ch]).start()

    def finish_early(c, _):
        rows = pl.ds(pl.multiple_of(c * 128, 128), 128)
        square = jnp.zeros((128, 128), F32)
        ms = []
        for p in range(PAIRS):
            cols = slice(p * 128, (p + 1) * 128)
            m = early_ref[rows, cols] + dot(earlyq_ref[rows, cols], cst_ref[p])
            ms.append(m)
            square = square + m * m
        scale = lax.rsqrt(jnp.sum(square, axis=1, keepdims=True) * (1.0 / D) + EPS)
        for p in range(PAIRS):
            y = ms[p] * scale * gain[:, p * 128:(p + 1) * 128]
            disp_send[0, pl.ds(c * 16, 16), p] = y.reshape(16, 8, 128).astype(BF16)
        return 0
    lax.fori_loop(0, M // 128, finish_early, 0)
    send_rows(0)

    def finish(c, _):
        rows = pl.ds(pl.multiple_of(c * C, C), C)
        square = jnp.zeros((C, 128), F32)
        for p in range(PAIRS):
            cols = slice(p * 128, (p + 1) * 128)
            m = mixed_ref[rows, cols] + dot(q_ref[rows, cols], cst_ref[p])
            mixed_ref[rows, cols] = m
            square = square + m * m
        scale = lax.rsqrt(jnp.sum(square, axis=1, keepdims=True) * (1.0 / D) + EPS)
        normed_ref[rows, :] = (mixed_ref[rows, :] * scale * gain).astype(BF16)
        return 0
    lax.fori_loop(0, NC, finish, 0)

    for ch in range(1, CH):
        this_pick = pick(ch)
        for n in range(3):
            y = dot(this_pick, normed_ref[:, n * 256:(n + 1) * 256])
            disp_send[ch, :, 2 * n] = y[:, :128].reshape(N, 8, 128).astype(BF16)
            disp_send[ch, :, 2 * n + 1] = y[:, 128:].reshape(N, 8, 128).astype(BF16)
        send_rows(ch)

    top = lax.broadcasted_iota(jnp.int32, (1, 8, 128), 1) < 4

    def ffn(e, start, rows, put):
        def first(f, _):
            hid = dot(a_ref[start:start + rows, :], win[e, :, lanes(f, 256)])
            h_ref[start:start + rows, lanes(f, 256)] = jnp.maximum(hid, 0.0).astype(BF16)
            return 0
        lax.fori_loop(0, FF // 256, first, 0)

        def second(n, _):
            put(n, dot(h_ref[start:start + rows, :], wout[e, :, lanes(n, 256)]))
            return 0
        lax.fori_loop(0, D // 256, second, 0)

    def bulk(buf, sem):
        return pltpu.make_async_copy(buf.at[pl.ds(0, N - 1)], buf.at[pl.ds(0, N - 1)], sem)

    for ch in range(CH):
        pltpu.make_async_copy(disp_send.at[ch, me], disp_recv.at[ch, me], self_sem.at[2 + ch]).wait()
        bulk(disp_recv.at[ch], disp_rsem.at[ch]).wait()
        if ch < 2:
            weights[2 * ch].wait()
            weights[2 * ch + 1].wait()
            for j in range(6):
                a_ref[:, j * 128:(j + 1) * 128] = disp_recv[ch, :, j].astype(F32).reshape(M, 128).astype(BF16)

            def put(n, o):
                ret_send[ch, :, 2 * n] = o[:, :128].reshape(N, 8, 128).astype(BF16)
                ret_send[ch, :, 2 * n + 1] = o[:, 128:].reshape(N, 8, 128).astype(BF16)
            ffn(ch, 0, M, put)
        else:
            for j in range(6):
                x = disp_recv[ch, :, j].astype(F32).reshape(N // 2, 2, 8, 128)
                even, odd = x[:, 0], x[:, 1]
                x0 = jnp.where(top, even, pltpu.roll(odd, 4, 1))
                x1 = jnp.where(top, pltpu.roll(even, 4, 1), odd)
                a_ref[:256, j * 128:(j + 1) * 128] = x0.reshape(256, 128).astype(BF16)
                a_ref[256:, j * 128:(j + 1) * 128] = x1.reshape(256, 128).astype(BF16)

            def put0(n, o):
                acc_ref[:256, lanes(n, 256)] = o

            def put1(n, o):
                acc_ref[256:512, lanes(n, 256)] = o
            ffn(0, 0, 256, put0)
            ffn(1, 256, 256, put1)
            for j in range(6):
                o0 = acc_ref[:256, j * 128:(j + 1) * 128].reshape(N // 2, 8, 128)
                o1 = acc_ref[256:512, j * 128:(j + 1) * 128].reshape(N // 2, 8, 128)
                even = jnp.where(top, o0, pltpu.roll(o1, 4, 1))
                odd = jnp.where(top, pltpu.roll(o0, 4, 1), o1)
                ret_send[ch, :, j] = jnp.stack([even, odd], axis=1).reshape(N, 8, 128).astype(BF16)

        for o in (MIXED if ch < 2 else ORDER):
            d = other(o)
            remote(ret_send.at[ch, d], ret_recv.at[ch, me], ret_ssem.at[ch], ret_rsem.at[ch], d).start()
        pltpu.make_async_copy(ret_send.at[ch, me], ret_recv.at[ch, me], self_sem.at[5 + ch]).start()

    for ch in range(CH):
        pltpu.make_async_copy(ret_send.at[ch, me], ret_recv.at[ch, me], self_sem.at[5 + ch]).wait()
        bulk(ret_recv.at[ch], ret_rsem.at[ch]).wait()
        for j in range(6):
            a_ref[:, j * 128:(j + 1) * 128] = ret_recv[ch, :, j].astype(F32).reshape(M, 128).astype(BF16)

        def unpack(c, _):
            rows = pl.ds(pl.multiple_of(c * C, C), C)
            back = spread(slot_ref[rows, :] - ch * M)
            for n in range(3):
                cols = slice(n * 256, (n + 1) * 256)
                y = dot(back, a_ref[:, cols])
                if ch == 0:
                    acc_ref[rows, cols] = y
                elif ch == 1:
                    acc_ref[rows, cols] = normed_ref[rows, cols].astype(F32) + (acc_ref[rows, cols] + y)
                else:
                    out_ref[rows, cols] = (acc_ref[rows, cols] + y).astype(BF16)
            return 0
        lax.fori_loop(0, NC, unpack, 0)

    @pl.when(me < OWN)
    def _():
        pltpu.make_async_copy(st_send.at[pl.ds(0, OWN - 1)], st_send.at[pl.ds(0, OWN - 1)], st_sem.at[0]).wait()
        bulk(pre_send, pre_sem.at[0]).wait()

    @pl.when(me >= OWN)
    def _():
        pltpu.make_async_copy(st_send, st_send, st_sem.at[0]).wait()
    for ch in range(CH):
        bulk(disp_send.at[ch], disp_ssem.at[ch]).wait()
        bulk(ret_send.at[ch], ret_ssem.at[ch]).wait()


def shards(queries, keys, values, norm_gain, expert_ids, w_in, w_out):
    hbm = pl.BlockSpec(memory_space=pltpu.HBM)
    vmem = pl.BlockSpec(memory_space=pltpu.VMEM)
    dma = pltpu.SemaphoreType.DMA
    return pl.pallas_call(
        body,
        out_shape=jax.ShapeDtypeStruct((T, D), BF16),
        in_specs=[hbm] * 7,
        out_specs=vmem,
        scratch_shapes=[
            pltpu.VMEM((D,), F32), pltpu.VMEM((1, T), jnp.int32),
            pltpu.VMEM((T, D), BF16), pltpu.VMEM((T, D), BF16), pltpu.VMEM((T, D), BF16),
            pltpu.VMEM((2, D, FF), BF16), pltpu.VMEM((2, FF, D), BF16),
            pltpu.VMEM((PAIRS, NC, 128, 128), F32), pltpu.VMEM((PAIRS, 128, 128), BF16),
            pltpu.VMEM((T, D), F32), pltpu.VMEM((T, D), BF16),
            pltpu.VMEM((OWN, 8, 128), BF16), pltpu.VMEM((N, 8, 128), BF16),
            pltpu.VMEM((N, 8, 128), BF16), pltpu.VMEM((OWN, 8, 128), BF16),
            pltpu.VMEM((T, 128), jnp.int32), pltpu.VMEM((M, D), F32), pltpu.VMEM((M, D), BF16),
            pltpu.VMEM((CH, N, 6, 8, 128), BF16), pltpu.VMEM((CH, N, 6, 8, 128), BF16),
            pltpu.VMEM((CH, N, 6, 8, 128), BF16), pltpu.VMEM((CH, N, 6, 8, 128), BF16),
            pltpu.VMEM((M, D), BF16), pltpu.VMEM((M, FF), BF16), pltpu.VMEM((T, D), F32),
            dma((5,)), dma((4,)), dma((8,)), dma((2,)), dma((2,)),
            dma((CH,)), dma((CH,)), dma((CH,)), dma((CH,)),
        ],
        compiler_params=pltpu.CompilerParams(
            collective_id=0, has_side_effects=True, vmem_limit_bytes=52 * 2**20),
        name="block",
    )(queries, keys, values, pltpu.with_memory_space_constraint(norm_gain, pltpu.HBM),
      pltpu.with_memory_space_constraint(expert_ids.reshape(1, T), pltpu.HBM), w_in, w_out)


def solution(mesh):
    rows = P(("dp", "seq"), None)
    weights = P(("dp", "seq"), None, None)
    return jax.shard_map(
        shards, mesh=mesh, in_specs=(rows, rows, rows, P(), rows, weights, weights),
        out_specs=rows, check_vma=False)
```

```python
import jax
import jax.numpy as jnp
from jax import lax
from jax.experimental import pallas as pl
from jax.experimental.pallas import tpu as pltpu
from jax.sharding import PartitionSpec as P

MESH = pl.DeviceIdType.MESH
EPS = 1e-06
F32 = jnp.float32
BF16 = jnp.bfloat16

N = 64
T = 1024
D = 768
FF = 3072
E = 128
PAIRS = 6
C = 256
NC = T // C
OWN = 24
CH = 3
M = 512


def hops(o):
    return sum((0, 1, 2, 1)[g] for g in (o // 16, o // 4 % 4, o % 4))


SPLIT = 4
ORDER = sorted(range(1, N), key=lambda o: (-hops(o), o * 37 % 64))
MIXED = [o * 21 % 64 for o in range(1, N)]

NEAR = [o for o in ORDER if hops(o) < 3]
MIDWAY = [o for o in ORDER if hops(o) == 3]


def dot(a, b):
    return jnp.dot(a, b, preferred_element_type=F32)


def dot_nt(a, b):
    return lax.dot_general(a, b, (((1,), (1,)), ((), ())), preferred_element_type=F32)


def dot_tn(a, b):
    return lax.dot_general(a, b, (((0,), (0,)), ((), ())), preferred_element_type=F32)


def lanes(p, width=128):
    return pl.ds(pl.multiple_of(p * width, width), width)


def spread(place):
    lane = lax.broadcasted_iota(jnp.int32, (1, 128), 1)
    return jnp.concatenate([jnp.where(place == lane + 128 * i, 1.0, 0.0).astype(BF16) for i in range(M // 128)], axis=1)


def body(q_hbm, k_hbm, v_hbm, gain_hbm, ids_hbm, win_hbm, wout_hbm,
         out_ref,
         gain_ref, ids_ref, q_ref, k_ref, v_ref, win, wout, kv_ref, cst_ref, mixed_ref, normed_ref,
         st_send, st_recv, pre_send, pre_recv, slot_ref, early_ref, earlyq_ref, disp_send, disp_recv, ret_send, ret_recv,
         a_ref, h_ref, acc_ref,
         ld_sem, w_sem, self_sem, st_sem, pre_sem, disp_ssem, disp_rsem, ret_ssem, ret_rsem):
    me = lax.axis_index("seq")
    my, mz, mx = me // 16, lax.rem(me // 4, 4), lax.rem(me, 4)
    ys = [lax.rem(my + g, 4) * 16 for g in range(4)]
    zs = [lax.rem(mz + g, 4) * 4 for g in range(4)]
    xs = [lax.rem(mx + g, 4) for g in range(4)]

    def other(o):
        return ys[o // 16] + zs[o // 4 % 4] + xs[o % 4]

    mine = jnp.where(my < 2, me, ys[2] + zs[2] + xs[2])

    def slice_of(o):
        far = ys[(o // 16 + 2) % 4] + zs[(o // 4 + 2) % 4] + xs[(o + 2) % 4]
        return jnp.where(other(o) < N // 2, other(o), far)

    def remote(src, dst, ssem, rsem, d):
        return pltpu.make_async_remote_copy(
            src_ref=src, dst_ref=dst, send_sem=ssem, recv_sem=rsem,
            device_id={"seq": d}, device_id_type=MESH)

    barrier = pltpu.get_barrier_semaphore()

    for o in ORDER:
        pl.semaphore_signal(barrier, inc=1, device_id={"seq": other(o)}, device_id_type=MESH)

    loads = [pltpu.make_async_copy(s, d, ld_sem.at[i])
             for i, (s, d) in enumerate(((k_hbm, k_ref), (v_hbm, v_ref), (ids_hbm, ids_ref), (gain_hbm, gain_ref), (q_hbm, q_ref)))]
    for c in loads:
        c.start()
    weights = [pltpu.make_async_copy(s.at[e], d.at[e], w_sem.at[2 * e + i])
               for e in range(2) for i, (s, d) in enumerate(((win_hbm, win), (wout_hbm, wout)))]
    for c in weights:
        c.start()

    lane = lax.broadcasted_iota(jnp.int32, (1, 128), 1)
    low = lane < 64

    loads[0].wait()
    loads[1].wait()
    row128 = lax.broadcasted_iota(jnp.int32, (128, 128), 0)
    lane128 = lax.broadcasted_iota(jnp.int32, (128, 128), 1)
    diag = (row128 < 64) == (lane128 < 64)

    def states(p, _):
        total = jnp.zeros((128, 128), F32)
        for c in range(NC):
            kv_ref[p, c] = total
            kc = k_ref[c * C:(c + 1) * C, lanes(p)]
            vc = v_ref[c * C:(c + 1) * C, lanes(p)]
            total = total + jnp.where(diag, dot_tn(kc, vc), 0.0)
        compact = jnp.where(low, total[:64], total[64:])
        st_send[pl.ds(p * 4, 4)] = compact.reshape(4, 2, 8, 128).astype(BF16)
        return 0
    lax.fori_loop(0, PAIRS, states, 0)

    loads[2].wait()
    loads[3].wait()
    ids = ids_ref[...]
    trib = jnp.where(lax.broadcasted_iota(jnp.int32, (C, C), 0) <= lax.broadcasted_iota(jnp.int32, (C, C), 1),
                     1.0, 0.0).astype(BF16)
    expert = lax.broadcasted_iota(jnp.int32, (E, C), 0)
    before = jnp.zeros((E, 1), F32)
    pieces = []
    for c in range(NC):
        idc = ids[:, c * C:(c + 1) * C]
        match = jnp.where(expert == idc, 1.0, 0.0)
        running = dot(match.astype(BF16), trib) + before
        rank = jnp.sum(running * match, axis=0, keepdims=True).astype(jnp.int32) - 1
        before = before + jnp.sum(match, axis=1, keepdims=True)
        half = lax.rem(idc, 2)
        owner = lax.div(idc, 2)
        pieces.append(jnp.where(rank < 8, half * M + owner * 8 + rank, 2 * M + owner * 8 + half * 4 + rank - 8))
    slot_row = jnp.concatenate(pieces, axis=1)
    slot_ref[...] = jnp.transpose(jnp.broadcast_to(slot_row.astype(F32), (128, T))).astype(jnp.int32)

    pl.semaphore_wait(barrier, N - 1)
    for o in ORDER:
        part = slice_of(o)

        @pl.when(part < OWN)
        def _(part=part, d=other(o)):
            remote(st_send.at[part], st_recv.at[me], st_sem.at[0], st_sem.at[1], d).start()

    @pl.when(mine < OWN)
    def _():
        pltpu.make_async_copy(st_send.at[mine], st_recv.at[me], self_sem.at[0]).start()

    loads[4].wait()
    tri = lax.broadcasted_iota(jnp.int32, (C, C), 0) >= lax.broadcasted_iota(jnp.int32, (C, C), 1)

    def local(p, _):
        for c in range(NC):
            rows = slice(c * C, (c + 1) * C)
            qc = q_ref[rows, lanes(p)]
            kc = k_ref[rows, lanes(p)]
            vc = v_ref[rows, lanes(p)]
            zero = jnp.zeros_like(kc)
            s0 = jnp.where(tri, dot_nt(qc, jnp.where(low, kc, zero)), 0.0).astype(BF16)
            s1 = jnp.where(tri, dot_nt(qc, jnp.where(low, zero, kc)), 0.0).astype(BF16)
            mixed_ref[rows, lanes(p)] = (dot(s0, jnp.where(low, vc, zero)) + dot(s1, jnp.where(low, zero, vc))
                                         + dot(qc, kv_ref[p, c].astype(BF16)))
        return 0
    lax.fori_loop(0, SPLIT, local, 0)

    @pl.when(mine < OWN)
    def _():
        pltpu.make_async_copy(st_send.at[mine], st_recv.at[me], self_sem.at[0]).wait()
        pltpu.make_async_copy(st_recv.at[pl.ds(0, N - 1)], st_recv.at[pl.ds(0, N - 1)], st_sem.at[1]).wait()

        def step(i, run):
            pre_send[i] = run.astype(BF16)
            return run + st_recv[i].astype(F32)
        lax.fori_loop(0, N, step, jnp.zeros((2, 8, 128), F32), unroll=8)

        for o in NEAR:
            d = other(o)
            remote(pre_send.at[d], pre_recv.at[mine], pre_sem.at[0], pre_sem.at[1], d).start()

        @pl.when(my < 2)
        def _():
            for o in MIDWAY:
                d = other(o)
                remote(pre_send.at[d], pre_recv.at[mine], pre_sem.at[0], pre_sem.at[1], d).start()
        pltpu.make_async_copy(pre_send.at[me], pre_recv.at[mine], self_sem.at[1]).start()

    lax.fori_loop(SPLIT, PAIRS, local, 0)

    def pick(ch):
        return jnp.where(lax.broadcasted_iota(jnp.int32, (M, T), 0) == slot_row - ch * M, 1.0, 0.0).astype(BF16)

    first_pick = pick(0)
    for n in range(3):
        cols = slice(n * 256, (n + 1) * 256)
        m = mixed_ref[:, cols]
        high = m.astype(BF16)
        early_ref[:, cols] = dot(first_pick, high) + dot(first_pick, (m - high.astype(F32)).astype(BF16))
        earlyq_ref[:, cols] = dot(first_pick, q_ref[:, cols]).astype(BF16)

    @pl.when(mine < OWN)
    def _():
        pltpu.make_async_copy(pre_send.at[me], pre_recv.at[mine], self_sem.at[1]).wait()
        pltpu.make_async_copy(pre_recv.at[pl.ds(0, OWN - 1)], pre_recv.at[pl.ds(0, OWN - 1)], pre_sem.at[1]).wait()

    @pl.when(mine >= OWN)
    def _():
        pltpu.make_async_copy(pre_recv, pre_recv, pre_sem.at[1]).wait()

    for p in range(PAIRS):
        compact = pre_recv[pl.ds(p * 4, 4)].astype(F32).reshape(64, 128)
        cst_ref[p, :64] = jnp.where(low, compact, 0.0).astype(BF16)
        cst_ref[p, 64:] = jnp.where(low, 0.0, compact).astype(BF16)

    gain = gain_ref[...].reshape(1, D)

    def send_rows(ch, offsets):
        for o in offsets:
            d = other(o)
            remote(disp_send.at[ch, d], disp_recv.at[ch, me], disp_ssem.at[ch], disp_rsem.at[ch], d).start()

    def keep_own(ch):
        pltpu.make_async_copy(disp_send.at[ch, me], disp_recv.at[ch, me], self_sem.at[2 + ch]).start()

    for g in (2, 1, 3, 0):
        rows = pl.ds(pl.multiple_of(ys[g] * 8, 128), 128)
        square = jnp.zeros((128, 128), F32)
        ms = []
        for p in range(PAIRS):
            cols = slice(p * 128, (p + 1) * 128)
            m = early_ref[rows, cols] + dot(earlyq_ref[rows, cols], cst_ref[p])
            ms.append(m)
            square = square + m * m
        scale = lax.rsqrt(jnp.sum(square, axis=1, keepdims=True) * (1.0 / D) + EPS)
        for p in range(PAIRS):
            y = ms[p] * scale * gain[:, p * 128:(p + 1) * 128]
            disp_send[0, pl.ds(ys[g], 16), p] = y.reshape(16, 8, 128).astype(BF16)
    send_rows(0, MIXED)
    keep_own(0)

    def finish(c, _):
        rows = pl.ds(pl.multiple_of(c * C, C), C)
        square = jnp.zeros((C, 128), F32)
        for p in range(PAIRS):
            cols = slice(p * 128, (p + 1) * 128)
            m = mixed_ref[rows, cols] + dot(q_ref[rows, cols], cst_ref[p])
            mixed_ref[rows, cols] = m
            square = square + m * m
        scale = lax.rsqrt(jnp.sum(square, axis=1, keepdims=True) * (1.0 / D) + EPS)
        normed_ref[rows, :] = (mixed_ref[rows, :] * scale * gain).astype(BF16)
        return 0
    lax.fori_loop(0, NC, finish, 0)

    for ch in range(1, CH):
        this_pick = pick(ch)
        for n in range(3):
            y = dot(this_pick, normed_ref[:, n * 256:(n + 1) * 256])
            disp_send[ch, :, 2 * n] = y[:, :128].reshape(N, 8, 128).astype(BF16)
            disp_send[ch, :, 2 * n + 1] = y[:, 128:].reshape(N, 8, 128).astype(BF16)
        send_rows(ch, MIXED)
        keep_own(ch)

    top = lax.broadcasted_iota(jnp.int32, (1, 8, 128), 1) < 4

    def ffn(e, start, rows, put):
        def first(f, _):
            hid = dot(a_ref[start:start + rows, :], win[e, :, lanes(f, 256)])
            h_ref[start:start + rows, lanes(f, 256)] = jnp.maximum(hid, 0.0).astype(BF16)
            return 0
        lax.fori_loop(0, FF // 256, first, 0)

        def second(n, _):
            put(n, dot(h_ref[start:start + rows, :], wout[e, :, lanes(n, 256)]))
            return 0
        lax.fori_loop(0, D // 256, second, 0)

    def bulk(buf, sem):
        return pltpu.make_async_copy(buf.at[pl.ds(0, N - 1)], buf.at[pl.ds(0, N - 1)], sem)

    for ch in range(CH):
        pltpu.make_async_copy(disp_send.at[ch, me], disp_recv.at[ch, me], self_sem.at[2 + ch]).wait()
        bulk(disp_recv.at[ch], disp_rsem.at[ch]).wait()
        if ch < 2:
            weights[2 * ch].wait()
            weights[2 * ch + 1].wait()
            for j in range(6):
                a_ref[:, j * 128:(j + 1) * 128] = disp_recv[ch, :, j].astype(F32).reshape(M, 128).astype(BF16)

            def put(n, o):
                ret_send[ch, :, 2 * n] = o[:, :128].reshape(N, 8, 128).astype(BF16)
                ret_send[ch, :, 2 * n + 1] = o[:, 128:].reshape(N, 8, 128).astype(BF16)
            ffn(ch, 0, M, put)
        else:
            for j in range(6):
                x = disp_recv[ch, :, j].astype(F32).reshape(N // 2, 2, 8, 128)
                even, odd = x[:, 0], x[:, 1]
                x0 = jnp.where(top, even, pltpu.roll(odd, 4, 1))
                x1 = jnp.where(top, pltpu.roll(even, 4, 1), odd)
                a_ref[:256, j * 128:(j + 1) * 128] = x0.reshape(256, 128).astype(BF16)
                a_ref[256:, j * 128:(j + 1) * 128] = x1.reshape(256, 128).astype(BF16)

            def put0(n, o):
                acc_ref[:256, lanes(n, 256)] = o

            def put1(n, o):
                acc_ref[256:512, lanes(n, 256)] = o
            ffn(0, 0, 256, put0)
            ffn(1, 256, 256, put1)
            for j in range(6):
                o0 = acc_ref[:256, j * 128:(j + 1) * 128].reshape(N // 2, 8, 128)
                o1 = acc_ref[256:512, j * 128:(j + 1) * 128].reshape(N // 2, 8, 128)
                even = jnp.where(top, o0, pltpu.roll(o1, 4, 1))
                odd = jnp.where(top, pltpu.roll(o0, 4, 1), o1)
                ret_send[ch, :, j] = jnp.stack([even, odd], axis=1).reshape(N, 8, 128).astype(BF16)

        for part in range(1 if ch < 2 else 2):
            cols = pl.ds(0, 6) if ch < 2 else pl.ds(3 * part, 3)
            for o in (MIXED if part == 0 else ORDER):
                d = other(o)
                remote(ret_send.at[ch, d, cols], ret_recv.at[ch, me, cols],
                       ret_ssem.at[ch], ret_rsem.at[ch + part], d).start()
        pltpu.make_async_copy(ret_send.at[ch, me], ret_recv.at[ch, me], self_sem.at[5 + ch]).start()

    def level(ch, js):
        for j in js:
            a_ref[:, j * 128:(j + 1) * 128] = ret_recv[ch, :, j].astype(F32).reshape(M, 128).astype(BF16)

    for ch in range(2):
        pltpu.make_async_copy(ret_send.at[ch, me], ret_recv.at[ch, me], self_sem.at[5 + ch]).wait()
        bulk(ret_recv.at[ch], ret_rsem.at[ch]).wait()
        level(ch, range(6))

        def unpack(c, _):
            rows = pl.ds(pl.multiple_of(c * C, C), C)
            back = spread(slot_ref[rows, :] - ch * M)
            for n in range(3):
                cols = slice(n * 256, (n + 1) * 256)
                y = dot(back, a_ref[:, cols])
                if ch == 0:
                    acc_ref[rows, cols] = y
                else:
                    acc_ref[rows, cols] = normed_ref[rows, cols].astype(F32) + (acc_ref[rows, cols] + y)
            return 0
        lax.fori_loop(0, NC, unpack, 0)

    for c in range(NC):
        h_ref[:C, c * M:(c + 1) * M] = spread(slot_ref[c * C:(c + 1) * C, :] - 2 * M)
    pltpu.make_async_copy(ret_send.at[2, me], ret_recv.at[2, me], self_sem.at[7]).wait()
    for part in range(2):
        got = ret_recv.at[2, pl.ds(0, N - 1), pl.ds(3 * part, 3)]
        pltpu.make_async_copy(got, got, ret_rsem.at[2 + part]).wait()
        level(2, range(3 * part, 3 * part + 3))
        for c in range(NC):
            rows = slice(c * C, (c + 1) * C)
            cols = slice(part * 384, (part + 1) * 384)
            y = dot(h_ref[:C, c * M:(c + 1) * M], a_ref[:, cols])
            out_ref[rows, cols] = (acc_ref[rows, cols] + y).astype(BF16)

    def left(buf, count, sem):
        pltpu.make_async_copy(buf.at[pl.ds(0, count)], buf.at[pl.ds(0, count)], sem).wait()

    @pl.when(mine < OWN)
    def _():
        left(st_recv, 2 * OWN - 1, st_sem.at[0])

        @pl.when(my < 2)
        def _():
            left(pre_send, len(NEAR) + len(MIDWAY), pre_sem.at[0])

        @pl.when(my >= 2)
        def _():
            left(pre_send, len(NEAR), pre_sem.at[0])

    @pl.when(mine >= OWN)
    def _():
        left(st_recv, 2 * OWN, st_sem.at[0])
    for ch in range(CH):
        bulk(disp_send.at[ch], disp_ssem.at[ch]).wait()
        bulk(ret_send.at[ch], ret_ssem.at[ch]).wait()


def shards(queries, keys, values, norm_gain, expert_ids, w_in, w_out):
    hbm = pl.BlockSpec(memory_space=pltpu.HBM)
    vmem = pl.BlockSpec(memory_space=pltpu.VMEM)
    dma = pltpu.SemaphoreType.DMA
    return pl.pallas_call(
        body,
        out_shape=jax.ShapeDtypeStruct((T, D), BF16),
        in_specs=[hbm] * 7,
        out_specs=vmem,
        scratch_shapes=[
            pltpu.VMEM((D,), F32), pltpu.VMEM((1, T), jnp.int32),
            pltpu.VMEM((T, D), BF16), pltpu.VMEM((T, D), BF16), pltpu.VMEM((T, D), BF16),
            pltpu.VMEM((2, D, FF), BF16), pltpu.VMEM((2, FF, D), BF16),
            pltpu.VMEM((PAIRS, NC, 128, 128), F32), pltpu.VMEM((PAIRS, 128, 128), BF16),
            pltpu.VMEM((T, D), F32), pltpu.VMEM((T, D), BF16),
            pltpu.VMEM((OWN, 2, 8, 128), BF16), pltpu.VMEM((N, 2, 8, 128), BF16),
            pltpu.VMEM((N, 2, 8, 128), BF16), pltpu.VMEM((OWN, 2, 8, 128), BF16),
            pltpu.VMEM((T, 128), jnp.int32), pltpu.VMEM((M, D), F32), pltpu.VMEM((M, D), BF16),
            pltpu.VMEM((CH, N, 6, 8, 128), BF16), pltpu.VMEM((CH, N, 6, 8, 128), BF16),
            pltpu.VMEM((CH, N, 6, 8, 128), BF16), pltpu.VMEM((CH, N, 6, 8, 128), BF16),
            pltpu.VMEM((M, D), BF16), pltpu.VMEM((M, FF), BF16), pltpu.VMEM((T, D), F32),
            dma((5,)), dma((4,)), dma((8,)), dma((2,)), dma((2,)),
            dma((CH,)), dma((CH,)), dma((CH,)), dma((CH + 1,)),
        ],
        compiler_params=pltpu.CompilerParams(
            collective_id=0, has_side_effects=True, vmem_limit_bytes=52 * 2**20),
        name="block",
    )(queries, keys, values, pltpu.with_memory_space_constraint(norm_gain, pltpu.HBM),
      pltpu.with_memory_space_constraint(expert_ids.reshape(1, T), pltpu.HBM), w_in, w_out)


def solution(mesh):
    rows = P(("dp", "seq"), None)
    weights = P(("dp", "seq"), None, None)
    return jax.shard_map(
        shards, mesh=mesh, in_specs=(rows, rows, rows, P(), rows, weights, weights),
        out_specs=rows, check_vma=False)
```

```python
import jax
import jax.numpy as jnp
from jax import lax
from jax.experimental import pallas as pl
from jax.experimental.pallas import tpu as pltpu
from jax.sharding import PartitionSpec as P

MESH = pl.DeviceIdType.MESH
EPS = 1e-06
F32 = jnp.float32
BF16 = jnp.bfloat16

N = 64
T = 1024
D = 768
FF = 3072
E = 128
PAIRS = 6
C = 256
NC = T // C
OWN = 24
CH = 3
M = 512


def hops(o):
    return sum((0, 1, 2, 1)[g] for g in (o // 16, o // 4 % 4, o % 4))


SPLIT = 4
ORDER = sorted(range(1, N), key=lambda o: (-hops(o), o * 37 % 64))
MIXED = [o * 21 % 64 for o in range(1, N)]

NEAR = [o for o in ORDER if hops(o) < 3]
MIDWAY = [o for o in ORDER if hops(o) == 3]


def dot(a, b):
    return jnp.dot(a, b, preferred_element_type=F32)


def dot_nt(a, b):
    return lax.dot_general(a, b, (((1,), (1,)), ((), ())), preferred_element_type=F32)


def dot_tn(a, b):
    return lax.dot_general(a, b, (((0,), (0,)), ((), ())), preferred_element_type=F32)


def lanes(p, width=128):
    return pl.ds(pl.multiple_of(p * width, width), width)


def spread(place):
    lane = lax.broadcasted_iota(jnp.int32, (1, 128), 1)
    return jnp.concatenate([jnp.where(place == lane + 128 * i, 1.0, 0.0).astype(BF16) for i in range(M // 128)], axis=1)


def body(q_hbm, k_hbm, v_hbm, gain_hbm, ids_hbm, win_hbm, wout_hbm,
         out_ref,
         gain_ref, ids_ref, q_ref, k_ref, v_ref, win, wout, kv_ref, cst_ref, mixed_ref, normed_ref,
         st_send, st_recv, pre_send, pre_recv, slot_ref, early_ref, earlyq_ref, disp_send, disp_recv, ret_send, ret_recv,
         a_ref, h_ref, acc_ref,
         ld_sem, w_sem, self_sem, st_sem, pre_sem, disp_ssem, disp_rsem, ret_ssem, ret_rsem):
    me = lax.axis_index("seq")
    my, mz, mx = me // 16, lax.rem(me // 4, 4), lax.rem(me, 4)
    ys = [lax.rem(my + g, 4) * 16 for g in range(4)]
    zs = [lax.rem(mz + g, 4) * 4 for g in range(4)]
    xs = [lax.rem(mx + g, 4) for g in range(4)]

    def other(o):
        return ys[o // 16] + zs[o // 4 % 4] + xs[o % 4]

    mine = jnp.where(my < 2, me, ys[2] + zs[2] + xs[2])

    def slice_of(o):
        far = ys[(o // 16 + 2) % 4] + zs[(o // 4 + 2) % 4] + xs[(o + 2) % 4]
        return jnp.where(other(o) < N // 2, other(o), far)

    def remote(src, dst, ssem, rsem, d):
        return pltpu.make_async_remote_copy(
            src_ref=src, dst_ref=dst, send_sem=ssem, recv_sem=rsem,
            device_id={"seq": d}, device_id_type=MESH)

    barrier = pltpu.get_barrier_semaphore()

    for o in ORDER:
        pl.semaphore_signal(barrier, inc=1, device_id={"seq": other(o)}, device_id_type=MESH)

    loads = [pltpu.make_async_copy(s, d, ld_sem.at[i])
             for i, (s, d) in enumerate(((k_hbm, k_ref), (v_hbm, v_ref), (ids_hbm, ids_ref), (gain_hbm, gain_ref), (q_hbm, q_ref)))]
    for c in loads:
        c.start()
    weights = [pltpu.make_async_copy(s.at[e], d.at[e], w_sem.at[2 * e + i])
               for e in range(2) for i, (s, d) in enumerate(((win_hbm, win), (wout_hbm, wout)))]

    lane = lax.broadcasted_iota(jnp.int32, (1, 128), 1)
    low = lane < 64

    loads[0].wait()
    loads[1].wait()
    row128 = lax.broadcasted_iota(jnp.int32, (128, 128), 0)
    lane128 = lax.broadcasted_iota(jnp.int32, (128, 128), 1)
    diag = (row128 < 64) == (lane128 < 64)

    def states(p, _):
        total = jnp.zeros((128, 128), F32)
        for c in range(NC):
            kv_ref[p, c] = total
            kc = k_ref[c * C:(c + 1) * C, lanes(p)]
            vc = v_ref[c * C:(c + 1) * C, lanes(p)]
            total = total + jnp.where(diag, dot_tn(kc, vc), 0.0)
        compact = jnp.where(low, total[:64], total[64:])
        st_send[pl.ds(p * 4, 4)] = compact.reshape(4, 2, 8, 128).astype(BF16)
        return 0
    lax.fori_loop(0, PAIRS, states, 0)

    loads[2].wait()
    loads[3].wait()
    ids = ids_ref[...]
    trib = jnp.where(lax.broadcasted_iota(jnp.int32, (C, C), 0) <= lax.broadcasted_iota(jnp.int32, (C, C), 1),
                     1.0, 0.0).astype(BF16)
    expert = lax.broadcasted_iota(jnp.int32, (E, C), 0)
    before = jnp.zeros((E, 1), F32)
    pieces = []
    for c in range(NC):
        idc = ids[:, c * C:(c + 1) * C]
        match = jnp.where(expert == idc, 1.0, 0.0)
        running = dot(match.astype(BF16), trib) + before
        rank = jnp.sum(running * match, axis=0, keepdims=True).astype(jnp.int32) - 1
        before = before + jnp.sum(match, axis=1, keepdims=True)
        half = lax.rem(idc, 2)
        owner = lax.div(idc, 2)
        pieces.append(jnp.where(rank < 8, half * M + owner * 8 + rank, 2 * M + owner * 8 + half * 4 + rank - 8))
    slot_row = jnp.concatenate(pieces, axis=1)
    slot_ref[...] = jnp.transpose(jnp.broadcast_to(slot_row.astype(F32), (128, T))).astype(jnp.int32)

    pl.semaphore_wait(barrier, N - 1)
    for o in ORDER:
        part = slice_of(o)

        @pl.when(part < OWN)
        def _(part=part, d=other(o)):
            remote(st_send.at[part], st_recv.at[me], st_sem.at[0], st_sem.at[1], d).start()

    @pl.when(mine < OWN)
    def _():
        pltpu.make_async_copy(st_send.at[mine], st_recv.at[me], self_sem.at[0]).start()

    loads[4].wait()
    for c in weights:
        c.start()
    tri = lax.broadcasted_iota(jnp.int32, (C, C), 0) >= lax.broadcasted_iota(jnp.int32, (C, C), 1)

    def local(p, _):
        for c in range(NC):
            rows = slice(c * C, (c + 1) * C)
            qc = q_ref[rows, lanes(p)]
            kc = k_ref[rows, lanes(p)]
            vc = v_ref[rows, lanes(p)]
            zero = jnp.zeros_like(kc)
            s0 = jnp.where(tri, dot_nt(qc, jnp.where(low, kc, zero)), 0.0).astype(BF16)
            s1 = jnp.where(tri, dot_nt(qc, jnp.where(low, zero, kc)), 0.0).astype(BF16)
            mixed_ref[rows, lanes(p)] = (dot(s0, jnp.where(low, vc, zero)) + dot(s1, jnp.where(low, zero, vc))
                                         + dot(qc, kv_ref[p, c].astype(BF16)))
        return 0
    lax.fori_loop(0, SPLIT, local, 0)

    @pl.when(mine < OWN)
    def _():
        pltpu.make_async_copy(st_send.at[mine], st_recv.at[me], self_sem.at[0]).wait()
        pltpu.make_async_copy(st_recv.at[pl.ds(0, N - 1)], st_recv.at[pl.ds(0, N - 1)], st_sem.at[1]).wait()

        def step(i, run):
            pre_send[i] = run.astype(BF16)
            return run + st_recv[i].astype(F32)
        lax.fori_loop(0, N, step, jnp.zeros((2, 8, 128), F32), unroll=8)

        for o in NEAR:
            d = other(o)
            remote(pre_send.at[d], pre_recv.at[mine], pre_sem.at[0], pre_sem.at[1], d).start()

        @pl.when(my < 2)
        def _():
            for o in MIDWAY:
                d = other(o)
                remote(pre_send.at[d], pre_recv.at[mine], pre_sem.at[0], pre_sem.at[1], d).start()
        pltpu.make_async_copy(pre_send.at[me], pre_recv.at[mine], self_sem.at[1]).start()

    lax.fori_loop(SPLIT, PAIRS, local, 0)

    def pick(ch):
        return jnp.where(lax.broadcasted_iota(jnp.int32, (M, T), 0) == slot_row - ch * M, 1.0, 0.0).astype(BF16)

    first_pick = pick(0)
    for n in range(3):
        cols = slice(n * 256, (n + 1) * 256)
        m = mixed_ref[:, cols]
        high = m.astype(BF16)
        early_ref[:, cols] = dot(first_pick, high) + dot(first_pick, (m - high.astype(F32)).astype(BF16))
        earlyq_ref[:, cols] = dot(first_pick, q_ref[:, cols]).astype(BF16)

    @pl.when(mine < OWN)
    def _():
        pltpu.make_async_copy(pre_send.at[me], pre_recv.at[mine], self_sem.at[1]).wait()
        pltpu.make_async_copy(pre_recv.at[pl.ds(0, OWN - 1)], pre_recv.at[pl.ds(0, OWN - 1)], pre_sem.at[1]).wait()

    @pl.when(mine >= OWN)
    def _():
        pltpu.make_async_copy(pre_recv, pre_recv, pre_sem.at[1]).wait()

    for p in range(PAIRS):
        compact = pre_recv[pl.ds(p * 4, 4)].astype(F32).reshape(64, 128)
        cst_ref[p, :64] = jnp.where(low, compact, 0.0).astype(BF16)
        cst_ref[p, 64:] = jnp.where(low, 0.0, compact).astype(BF16)

    gain = gain_ref[...].reshape(1, D)

    def send_rows(ch, offsets):
        for o in offsets:
            d = other(o)
            remote(disp_send.at[ch, d], disp_recv.at[ch, me], disp_ssem.at[ch], disp_rsem.at[ch], d).start()

    def keep_own(ch):
        pltpu.make_async_copy(disp_send.at[ch, me], disp_recv.at[ch, me], self_sem.at[2 + ch]).start()

    for g in (2, 1, 3, 0):
        rows = pl.ds(pl.multiple_of(ys[g] * 8, 128), 128)
        square = jnp.zeros((128, 128), F32)
        ms = []
        for p in range(PAIRS):
            cols = slice(p * 128, (p + 1) * 128)
            m = early_ref[rows, cols] + dot(earlyq_ref[rows, cols], cst_ref[p])
            ms.append(m)
            square = square + m * m
        scale = lax.rsqrt(jnp.sum(square, axis=1, keepdims=True) * (1.0 / D) + EPS)
        for p in range(PAIRS):
            y = ms[p] * scale * gain[:, p * 128:(p + 1) * 128]
            disp_send[0, pl.ds(ys[g], 16), p] = y.reshape(16, 8, 128).astype(BF16)
    send_rows(0, MIXED)
    keep_own(0)

    def finish(c, _):
        rows = pl.ds(pl.multiple_of(c * C, C), C)
        square = jnp.zeros((C, 128), F32)
        for p in range(PAIRS):
            cols = slice(p * 128, (p + 1) * 128)
            m = mixed_ref[rows, cols] + dot(q_ref[rows, cols], cst_ref[p])
            mixed_ref[rows, cols] = m
            square = square + m * m
        scale = lax.rsqrt(jnp.sum(square, axis=1, keepdims=True) * (1.0 / D) + EPS)
        normed_ref[rows, :] = (mixed_ref[rows, :] * scale * gain).astype(BF16)
        return 0
    lax.fori_loop(0, NC, finish, 0)

    for ch in range(1, CH):
        this_pick = pick(ch)
        for n in range(3):
            y = dot(this_pick, normed_ref[:, n * 256:(n + 1) * 256])
            disp_send[ch, :, 2 * n] = y[:, :128].reshape(N, 8, 128).astype(BF16)
            disp_send[ch, :, 2 * n + 1] = y[:, 128:].reshape(N, 8, 128).astype(BF16)
        send_rows(ch, MIXED)
        keep_own(ch)

    top = lax.broadcasted_iota(jnp.int32, (1, 8, 128), 1) < 4

    def ffn(e, start, rows, put):
        def first(f, _):
            hid = dot(a_ref[start:start + rows, :], win[e, :, lanes(f, 256)])
            h_ref[start:start + rows, lanes(f, 256)] = jnp.maximum(hid, 0.0).astype(BF16)
            return 0
        lax.fori_loop(0, FF // 256, first, 0)

        def second(n, _):
            put(n, dot(h_ref[start:start + rows, :], wout[e, :, lanes(n, 256)]))
            return 0
        lax.fori_loop(0, D // 256, second, 0)

    def bulk(buf, sem):
        return pltpu.make_async_copy(buf.at[pl.ds(0, N - 1)], buf.at[pl.ds(0, N - 1)], sem)

    for ch in range(CH):
        pltpu.make_async_copy(disp_send.at[ch, me], disp_recv.at[ch, me], self_sem.at[2 + ch]).wait()
        bulk(disp_recv.at[ch], disp_rsem.at[ch]).wait()
        if ch < 2:
            weights[2 * ch].wait()
            weights[2 * ch + 1].wait()
            for j in range(6):
                a_ref[:, j * 128:(j + 1) * 128] = disp_recv[ch, :, j].astype(F32).reshape(M, 128).astype(BF16)

            def put(n, o):
                ret_send[ch, :, 2 * n] = o[:, :128].reshape(N, 8, 128).astype(BF16)
                ret_send[ch, :, 2 * n + 1] = o[:, 128:].reshape(N, 8, 128).astype(BF16)
            ffn(ch, 0, M, put)
        else:
            for j in range(6):
                x = disp_recv[ch, :, j].astype(F32).reshape(N // 2, 2, 8, 128)
                even, odd = x[:, 0], x[:, 1]
                x0 = jnp.where(top, even, pltpu.roll(odd, 4, 1))
                x1 = jnp.where(top, pltpu.roll(even, 4, 1), odd)
                a_ref[:256, j * 128:(j + 1) * 128] = x0.reshape(256, 128).astype(BF16)
                a_ref[256:, j * 128:(j + 1) * 128] = x1.reshape(256, 128).astype(BF16)

            def put0(n, o):
                acc_ref[:256, lanes(n, 256)] = o

            def put1(n, o):
                acc_ref[256:512, lanes(n, 256)] = o
            ffn(0, 0, 256, put0)
            ffn(1, 256, 256, put1)
            for j in range(6):
                o0 = acc_ref[:256, j * 128:(j + 1) * 128].reshape(N // 2, 8, 128)
                o1 = acc_ref[256:512, j * 128:(j + 1) * 128].reshape(N // 2, 8, 128)
                even = jnp.where(top, o0, pltpu.roll(o1, 4, 1))
                odd = jnp.where(top, pltpu.roll(o0, 4, 1), o1)
                ret_send[ch, :, j] = jnp.stack([even, odd], axis=1).reshape(N, 8, 128).astype(BF16)

        def give(d, cols, sem):
            remote(ret_send.at[ch, d, cols], ret_recv.at[ch, me, cols], ret_ssem.at[ch], ret_rsem.at[sem], d).start()

        if ch < 2:
            for o in MIXED:
                give(other(o), pl.ds(0, 6), ch)
        else:
            for o in MIXED:
                d = other(o)
                give(d, pl.ds(0, 3), ch)

                @pl.when(jnp.logical_or(ys[o // 16] == 0, zs[o // 4 % 4] == 0))
                def _(d=d):
                    give(d, pl.ds(3, 3), ch + 1)
            for o in ORDER:
                @pl.when(jnp.logical_not(jnp.logical_or(ys[o // 16] == 0, zs[o // 4 % 4] == 0)))
                def _(d=other(o)):
                    give(d, pl.ds(3, 3), ch + 1)
        pltpu.make_async_copy(ret_send.at[ch, me], ret_recv.at[ch, me], self_sem.at[5 + ch]).start()

    def level(ch, js):
        for j in js:
            a_ref[:, j * 128:(j + 1) * 128] = ret_recv[ch, :, j].astype(F32).reshape(M, 128).astype(BF16)

    for ch in range(2):
        pltpu.make_async_copy(ret_send.at[ch, me], ret_recv.at[ch, me], self_sem.at[5 + ch]).wait()
        bulk(ret_recv.at[ch], ret_rsem.at[ch]).wait()
        level(ch, range(6))

        def unpack(c, _):
            rows = pl.ds(pl.multiple_of(c * C, C), C)
            back = spread(slot_ref[rows, :] - ch * M)
            for n in range(3):
                cols = slice(n * 256, (n + 1) * 256)
                y = dot(back, a_ref[:, cols])
                if ch == 0:
                    acc_ref[rows, cols] = y
                else:
                    acc_ref[rows, cols] = normed_ref[rows, cols].astype(F32) + (acc_ref[rows, cols] + y)
            return 0
        lax.fori_loop(0, NC, unpack, 0)

    for c in range(NC):
        h_ref[:C, c * M:(c + 1) * M] = spread(slot_ref[c * C:(c + 1) * C, :] - 2 * M)
    pltpu.make_async_copy(ret_send.at[2, me], ret_recv.at[2, me], self_sem.at[7]).wait()
    for part in range(2):
        got = ret_recv.at[2, pl.ds(0, N - 1), pl.ds(3 * part, 3)]
        pltpu.make_async_copy(got, got, ret_rsem.at[2 + part]).wait()
        level(2, range(3 * part, 3 * part + 3))
        for c in range(NC):
            rows = slice(c * C, (c + 1) * C)
            cols = slice(part * 384, (part + 1) * 384)
            y = dot(h_ref[:C, c * M:(c + 1) * M], a_ref[:, cols])
            out_ref[rows, cols] = (acc_ref[rows, cols] + y).astype(BF16)

    def left(buf, count, sem):
        pltpu.make_async_copy(buf.at[pl.ds(0, count)], buf.at[pl.ds(0, count)], sem).wait()

    @pl.when(mine < OWN)
    def _():
        left(st_recv, 2 * OWN - 1, st_sem.at[0])

        @pl.when(my < 2)
        def _():
            left(pre_send, len(NEAR) + len(MIDWAY), pre_sem.at[0])

        @pl.when(my >= 2)
        def _():
            left(pre_send, len(NEAR), pre_sem.at[0])

    @pl.when(mine >= OWN)
    def _():
        left(st_recv, 2 * OWN, st_sem.at[0])
    for ch in range(CH):
        bulk(disp_send.at[ch], disp_ssem.at[ch]).wait()
        bulk(ret_send.at[ch], ret_ssem.at[ch]).wait()


def shards(queries, keys, values, norm_gain, expert_ids, w_in, w_out):
    hbm = pl.BlockSpec(memory_space=pltpu.HBM)
    vmem = pl.BlockSpec(memory_space=pltpu.VMEM)
    dma = pltpu.SemaphoreType.DMA
    return pl.pallas_call(
        body,
        out_shape=jax.ShapeDtypeStruct((T, D), BF16),
        in_specs=[hbm] * 7,
        out_specs=vmem,
        scratch_shapes=[
            pltpu.VMEM((D,), F32), pltpu.VMEM((1, T), jnp.int32),
            pltpu.VMEM((T, D), BF16), pltpu.VMEM((T, D), BF16), pltpu.VMEM((T, D), BF16),
            pltpu.VMEM((2, D, FF), BF16), pltpu.VMEM((2, FF, D), BF16),
            pltpu.VMEM((PAIRS, NC, 128, 128), F32), pltpu.VMEM((PAIRS, 128, 128), BF16),
            pltpu.VMEM((T, D), F32), pltpu.VMEM((T, D), BF16),
            pltpu.VMEM((OWN, 2, 8, 128), BF16), pltpu.VMEM((N, 2, 8, 128), BF16),
            pltpu.VMEM((N, 2, 8, 128), BF16), pltpu.VMEM((OWN, 2, 8, 128), BF16),
            pltpu.VMEM((T, 128), jnp.int32), pltpu.VMEM((M, D), F32), pltpu.VMEM((M, D), BF16),
            pltpu.VMEM((CH, N, 6, 8, 128), BF16), pltpu.VMEM((CH, N, 6, 8, 128), BF16),
            pltpu.VMEM((CH, N, 6, 8, 128), BF16), pltpu.VMEM((CH, N, 6, 8, 128), BF16),
            pltpu.VMEM((M, D), BF16), pltpu.VMEM((M, FF), BF16), pltpu.VMEM((T, D), F32),
            dma((5,)), dma((4,)), dma((8,)), dma((2,)), dma((2,)),
            dma((CH,)), dma((CH,)), dma((CH,)), dma((CH + 1,)),
        ],
        compiler_params=pltpu.CompilerParams(
            collective_id=0, has_side_effects=True, vmem_limit_bytes=52 * 2**20),
        name="block",
    )(queries, keys, values, pltpu.with_memory_space_constraint(norm_gain, pltpu.HBM),
      pltpu.with_memory_space_constraint(expert_ids.reshape(1, T), pltpu.HBM), w_in, w_out)


def solution(mesh):
    rows = P(("dp", "seq"), None)
    weights = P(("dp", "seq"), None, None)
    return jax.shard_map(
        shards, mesh=mesh, in_specs=(rows, rows, rows, P(), rows, weights, weights),
        out_specs=rows, check_vma=False)
```

```python
import jax
import jax.numpy as jnp
from jax import lax
from jax.experimental import pallas as pl
from jax.experimental.pallas import tpu as pltpu
from jax.sharding import PartitionSpec as P

MESH = pl.DeviceIdType.MESH
EPS = 1e-06
F32 = jnp.float32
BF16 = jnp.bfloat16

N = 64
T = 1024
D = 768
FF = 3072
E = 128
PAIRS = 6
C = 256
NC = T // C
OWN = 24
CH = 3
M = 512


def hops(o):
    return sum((0, 1, 2, 1)[g] for g in (o // 16, o // 4 % 4, o % 4))


SPLIT = 4
ORDER = sorted(range(1, N), key=lambda o: (-hops(o), o * 37 % 64))
MIXED = [o * 21 % 64 for o in range(1, N)]

NEAR = [o for o in ORDER if hops(o) < 3]
MIDWAY = [o for o in ORDER if hops(o) == 3]


def dot(a, b):
    return jnp.dot(a, b, preferred_element_type=F32)


def dot_nt(a, b):
    return lax.dot_general(a, b, (((1,), (1,)), ((), ())), preferred_element_type=F32)


def dot_tn(a, b):
    return lax.dot_general(a, b, (((0,), (0,)), ((), ())), preferred_element_type=F32)


def lanes(p, width=128):
    return pl.ds(pl.multiple_of(p * width, width), width)


def spread(place):
    lane = lax.broadcasted_iota(jnp.int32, (1, 128), 1)
    return jnp.concatenate([jnp.where(place == lane + 128 * i, 1.0, 0.0).astype(BF16) for i in range(M // 128)], axis=1)


def body(q_hbm, k_hbm, v_hbm, gain_hbm, ids_hbm, win_hbm, wout_hbm,
         out_ref,
         gain_ref, ids_ref, q_ref, k_ref, v_ref, win, wout, kv_ref, cst_ref, mixed_ref, normed_ref,
         st_send, st_recv, pre_send, pre_recv, slot_ref, early_ref, earlyq_ref, disp_send, disp_recv, ret_send, ret_recv,
         a_ref, h_ref, acc_ref,
         ld_sem, w_sem, self_sem, st_sem, pre_sem, disp_ssem, disp_rsem, ret_ssem, ret_rsem):
    me = lax.axis_index("seq")
    my, mz, mx = me // 16, lax.rem(me // 4, 4), lax.rem(me, 4)
    turn = 1 + 2 * lax.axis_index("dp")
    ys = [lax.rem(my + g * turn, 4) * 16 for g in range(4)]
    zs = [lax.rem(mz + g * turn, 4) * 4 for g in range(4)]
    xs = [lax.rem(mx + g * turn, 4) for g in range(4)]

    def other(o):
        return ys[o // 16] + zs[o // 4 % 4] + xs[o % 4]

    mine = jnp.where(my < 2, me, ys[2] + zs[2] + xs[2])

    def slice_of(o):
        far = ys[(o // 16 + 2) % 4] + zs[(o // 4 + 2) % 4] + xs[(o + 2) % 4]
        return jnp.where(other(o) < N // 2, other(o), far)

    def remote(src, dst, ssem, rsem, d):
        return pltpu.make_async_remote_copy(
            src_ref=src, dst_ref=dst, send_sem=ssem, recv_sem=rsem,
            device_id={"seq": d}, device_id_type=MESH)

    barrier = pltpu.get_barrier_semaphore()

    for o in ORDER:
        pl.semaphore_signal(barrier, inc=1, device_id={"seq": other(o)}, device_id_type=MESH)

    loads = [pltpu.make_async_copy(s, d, ld_sem.at[i])
             for i, (s, d) in enumerate(((k_hbm, k_ref), (v_hbm, v_ref), (ids_hbm, ids_ref), (gain_hbm, gain_ref), (q_hbm, q_ref)))]
    for c in loads:
        c.start()
    weights = [pltpu.make_async_copy(s.at[e], d.at[e], w_sem.at[2 * e + i])
               for e in range(2) for i, (s, d) in enumerate(((win_hbm, win), (wout_hbm, wout)))]

    lane = lax.broadcasted_iota(jnp.int32, (1, 128), 1)
    low = lane < 64

    loads[0].wait()
    loads[1].wait()
    row128 = lax.broadcasted_iota(jnp.int32, (128, 128), 0)
    lane128 = lax.broadcasted_iota(jnp.int32, (128, 128), 1)
    diag = (row128 < 64) == (lane128 < 64)

    def states(p, _):
        total = jnp.zeros((128, 128), F32)
        for c in range(NC):
            kv_ref[p, c] = total
            kc = k_ref[c * C:(c + 1) * C, lanes(p)]
            vc = v_ref[c * C:(c + 1) * C, lanes(p)]
            total = total + jnp.where(diag, dot_tn(kc, vc), 0.0)
        compact = jnp.where(low, total[:64], total[64:])
        st_send[pl.ds(p * 4, 4)] = compact.reshape(4, 2, 8, 128).astype(BF16)
        return 0
    lax.fori_loop(0, PAIRS, states, 0)

    loads[2].wait()
    loads[3].wait()
    ids = ids_ref[...]
    trib = jnp.where(lax.broadcasted_iota(jnp.int32, (C, C), 0) <= lax.broadcasted_iota(jnp.int32, (C, C), 1),
                     1.0, 0.0).astype(BF16)
    expert = lax.broadcasted_iota(jnp.int32, (E, C), 0)
    before = jnp.zeros((E, 1), F32)
    pieces = []
    for c in range(NC):
        idc = ids[:, c * C:(c + 1) * C]
        match = jnp.where(expert == idc, 1.0, 0.0)
        running = dot(match.astype(BF16), trib) + before
        rank = jnp.sum(running * match, axis=0, keepdims=True).astype(jnp.int32) - 1
        before = before + jnp.sum(match, axis=1, keepdims=True)
        half = lax.rem(idc, 2)
        owner = lax.div(idc, 2)
        pieces.append(jnp.where(rank < 8, half * M + owner * 8 + rank, 2 * M + owner * 8 + half * 4 + rank - 8))
    slot_row = jnp.concatenate(pieces, axis=1)
    slot_ref[...] = jnp.transpose(jnp.broadcast_to(slot_row.astype(F32), (128, T))).astype(jnp.int32)

    pl.semaphore_wait(barrier, N - 1)
    for o in ORDER:
        part = slice_of(o)

        @pl.when(part < OWN)
        def _(part=part, d=other(o)):
            remote(st_send.at[part], st_recv.at[me], st_sem.at[0], st_sem.at[1], d).start()

    @pl.when(mine < OWN)
    def _():
        pltpu.make_async_copy(st_send.at[mine], st_recv.at[me], self_sem.at[0]).start()

    loads[4].wait()
    for c in weights:
        c.start()
    tri = lax.broadcasted_iota(jnp.int32, (C, C), 0) >= lax.broadcasted_iota(jnp.int32, (C, C), 1)

    def local(p, _):
        for c in range(NC):
            rows = slice(c * C, (c + 1) * C)
            qc = q_ref[rows, lanes(p)]
            kc = k_ref[rows, lanes(p)]
            vc = v_ref[rows, lanes(p)]
            zero = jnp.zeros_like(kc)
            s0 = jnp.where(tri, dot_nt(qc, jnp.where(low, kc, zero)), 0.0).astype(BF16)
            s1 = jnp.where(tri, dot_nt(qc, jnp.where(low, zero, kc)), 0.0).astype(BF16)
            mixed_ref[rows, lanes(p)] = (dot(s0, jnp.where(low, vc, zero)) + dot(s1, jnp.where(low, zero, vc))
                                         + dot(qc, kv_ref[p, c].astype(BF16)))
        return 0
    lax.fori_loop(0, SPLIT, local, 0)

    @pl.when(mine < OWN)
    def _():
        pltpu.make_async_copy(st_send.at[mine], st_recv.at[me], self_sem.at[0]).wait()
        pltpu.make_async_copy(st_recv.at[pl.ds(0, N - 1)], st_recv.at[pl.ds(0, N - 1)], st_sem.at[1]).wait()

        def step(i, run):
            pre_send[i] = run.astype(BF16)
            return run + st_recv[i].astype(F32)
        lax.fori_loop(0, N, step, jnp.zeros((2, 8, 128), F32), unroll=8)

        for o in NEAR:
            d = other(o)
            remote(pre_send.at[d], pre_recv.at[mine], pre_sem.at[0], pre_sem.at[1], d).start()

        @pl.when(my < 2)
        def _():
            for o in MIDWAY:
                d = other(o)
                remote(pre_send.at[d], pre_recv.at[mine], pre_sem.at[0], pre_sem.at[1], d).start()
        pltpu.make_async_copy(pre_send.at[me], pre_recv.at[mine], self_sem.at[1]).start()

    lax.fori_loop(SPLIT, PAIRS, local, 0)

    def pick(ch):
        return jnp.where(lax.broadcasted_iota(jnp.int32, (M, T), 0) == slot_row - ch * M, 1.0, 0.0).astype(BF16)

    first_pick = pick(0)
    for n in range(3):
        cols = slice(n * 256, (n + 1) * 256)
        m = mixed_ref[:, cols]
        high = m.astype(BF16)
        early_ref[:, cols] = dot(first_pick, high) + dot(first_pick, (m - high.astype(F32)).astype(BF16))
        earlyq_ref[:, cols] = dot(first_pick, q_ref[:, cols]).astype(BF16)

    @pl.when(mine < OWN)
    def _():
        pltpu.make_async_copy(pre_send.at[me], pre_recv.at[mine], self_sem.at[1]).wait()
        pltpu.make_async_copy(pre_recv.at[pl.ds(0, OWN - 1)], pre_recv.at[pl.ds(0, OWN - 1)], pre_sem.at[1]).wait()

    @pl.when(mine >= OWN)
    def _():
        pltpu.make_async_copy(pre_recv, pre_recv, pre_sem.at[1]).wait()

    for p in range(PAIRS):
        compact = pre_recv[pl.ds(p * 4, 4)].astype(F32).reshape(64, 128)
        cst_ref[p, :64] = jnp.where(low, compact, 0.0).astype(BF16)
        cst_ref[p, 64:] = jnp.where(low, 0.0, compact).astype(BF16)

    gain = gain_ref[...].reshape(1, D)

    def send_rows(ch, offsets):
        for o in offsets:
            d = other(o)
            remote(disp_send.at[ch, d], disp_recv.at[ch, me], disp_ssem.at[ch], disp_rsem.at[ch], d).start()

    def keep_own(ch):
        pltpu.make_async_copy(disp_send.at[ch, me], disp_recv.at[ch, me], self_sem.at[2 + ch]).start()

    for g in (2, 1, 3, 0):
        rows = pl.ds(pl.multiple_of(ys[g] * 8, 128), 128)
        square = jnp.zeros((128, 128), F32)
        ms = []
        for p in range(PAIRS):
            cols = slice(p * 128, (p + 1) * 128)
            m = early_ref[rows, cols] + dot(earlyq_ref[rows, cols], cst_ref[p])
            ms.append(m)
            square = square + m * m
        scale = lax.rsqrt(jnp.sum(square, axis=1, keepdims=True) * (1.0 / D) + EPS)
        for p in range(PAIRS):
            y = ms[p] * scale * gain[:, p * 128:(p + 1) * 128]
            disp_send[0, pl.ds(ys[g], 16), p] = y.reshape(16, 8, 128).astype(BF16)
    send_rows(0, MIXED)
    keep_own(0)

    def finish(c, _):
        rows = pl.ds(pl.multiple_of(c * C, C), C)
        square = jnp.zeros((C, 128), F32)
        for p in range(PAIRS):
            cols = slice(p * 128, (p + 1) * 128)
            m = mixed_ref[rows, cols] + dot(q_ref[rows, cols], cst_ref[p])
            mixed_ref[rows, cols] = m
            square = square + m * m
        scale = lax.rsqrt(jnp.sum(square, axis=1, keepdims=True) * (1.0 / D) + EPS)
        normed_ref[rows, :] = (mixed_ref[rows, :] * scale * gain).astype(BF16)
        return 0
    lax.fori_loop(0, NC, finish, 0)

    for ch in range(1, CH):
        this_pick = pick(ch)
        for n in range(3):
            y = dot(this_pick, normed_ref[:, n * 256:(n + 1) * 256])
            disp_send[ch, :, 2 * n] = y[:, :128].reshape(N, 8, 128).astype(BF16)
            disp_send[ch, :, 2 * n + 1] = y[:, 128:].reshape(N, 8, 128).astype(BF16)
        send_rows(ch, MIXED)
        keep_own(ch)

    top = lax.broadcasted_iota(jnp.int32, (1, 8, 128), 1) < 4

    def ffn(e, start, rows, put):
        def first(f, _):
            hid = dot(a_ref[start:start + rows, :], win[e, :, lanes(f, 256)])
            h_ref[start:start + rows, lanes(f, 256)] = jnp.maximum(hid, 0.0).astype(BF16)
            return 0
        lax.fori_loop(0, FF // 256, first, 0)

        def second(n, _):
            put(n, dot(h_ref[start:start + rows, :], wout[e, :, lanes(n, 256)]))
            return 0
        lax.fori_loop(0, D // 256, second, 0)

    def bulk(buf, sem):
        return pltpu.make_async_copy(buf.at[pl.ds(0, N - 1)], buf.at[pl.ds(0, N - 1)], sem)

    for ch in range(CH):
        pltpu.make_async_copy(disp_send.at[ch, me], disp_recv.at[ch, me], self_sem.at[2 + ch]).wait()
        bulk(disp_recv.at[ch], disp_rsem.at[ch]).wait()
        if ch < 2:
            weights[2 * ch].wait()
            weights[2 * ch + 1].wait()
            for j in range(6):
                a_ref[:, j * 128:(j + 1) * 128] = disp_recv[ch, :, j].astype(F32).reshape(M, 128).astype(BF16)

            def put(n, o):
                ret_send[ch, :, 2 * n] = o[:, :128].reshape(N, 8, 128).astype(BF16)
                ret_send[ch, :, 2 * n + 1] = o[:, 128:].reshape(N, 8, 128).astype(BF16)
            ffn(ch, 0, M, put)
        else:
            for j in range(6):
                x = disp_recv[ch, :, j].astype(F32).reshape(N // 2, 2, 8, 128)
                even, odd = x[:, 0], x[:, 1]
                x0 = jnp.where(top, even, pltpu.roll(odd, 4, 1))
                x1 = jnp.where(top, pltpu.roll(even, 4, 1), odd)
                a_ref[:256, j * 128:(j + 1) * 128] = x0.reshape(256, 128).astype(BF16)
                a_ref[256:, j * 128:(j + 1) * 128] = x1.reshape(256, 128).astype(BF16)

            def put0(n, o):
                acc_ref[:256, lanes(n, 256)] = o

            def put1(n, o):
                acc_ref[256:512, lanes(n, 256)] = o
            ffn(0, 0, 256, put0)
            ffn(1, 256, 256, put1)
            for j in range(6):
                o0 = acc_ref[:256, j * 128:(j + 1) * 128].reshape(N // 2, 8, 128)
                o1 = acc_ref[256:512, j * 128:(j + 1) * 128].reshape(N // 2, 8, 128)
                even = jnp.where(top, o0, pltpu.roll(o1, 4, 1))
                odd = jnp.where(top, pltpu.roll(o0, 4, 1), o1)
                ret_send[ch, :, j] = jnp.stack([even, odd], axis=1).reshape(N, 8, 128).astype(BF16)

        def give(d, cols, sem):
            remote(ret_send.at[ch, d, cols], ret_recv.at[ch, me, cols], ret_ssem.at[ch], ret_rsem.at[sem], d).start()

        if ch < 2:
            for o in MIXED:
                give(other(o), pl.ds(0, 6), ch)
        else:
            for o in MIXED:
                d = other(o)
                give(d, pl.ds(0, 3), ch)

                @pl.when(jnp.logical_or(ys[o // 16] == 0, zs[o // 4 % 4] == 0))
                def _(d=d):
                    give(d, pl.ds(3, 3), ch + 1)
            for o in ORDER:
                @pl.when(jnp.logical_not(jnp.logical_or(ys[o // 16] == 0, zs[o // 4 % 4] == 0)))
                def _(d=other(o)):
                    give(d, pl.ds(3, 3), ch + 1)
        pltpu.make_async_copy(ret_send.at[ch, me], ret_recv.at[ch, me], self_sem.at[5 + ch]).start()

    def level(ch, js):
        for j in js:
            a_ref[:, j * 128:(j + 1) * 128] = ret_recv[ch, :, j].astype(F32).reshape(M, 128).astype(BF16)

    for ch in range(2):
        pltpu.make_async_copy(ret_send.at[ch, me], ret_recv.at[ch, me], self_sem.at[5 + ch]).wait()
        bulk(ret_recv.at[ch], ret_rsem.at[ch]).wait()
        level(ch, range(6))

        def unpack(c, _):
            rows = pl.ds(pl.multiple_of(c * C, C), C)
            back = spread(slot_ref[rows, :] - ch * M)
            for n in range(3):
                cols = slice(n * 256, (n + 1) * 256)
                y = dot(back, a_ref[:, cols])
                if ch == 0:
                    acc_ref[rows, cols] = y
                else:
                    acc_ref[rows, cols] = normed_ref[rows, cols].astype(F32) + (acc_ref[rows, cols] + y)
            return 0
        lax.fori_loop(0, NC, unpack, 0)

    for c in range(NC):
        h_ref[:C, c * M:(c + 1) * M] = spread(slot_ref[c * C:(c + 1) * C, :] - 2 * M)
    pltpu.make_async_copy(ret_send.at[2, me], ret_recv.at[2, me], self_sem.at[7]).wait()
    for part in range(2):
        got = ret_recv.at[2, pl.ds(0, N - 1), pl.ds(3 * part, 3)]
        pltpu.make_async_copy(got, got, ret_rsem.at[2 + part]).wait()
        level(2, range(3 * part, 3 * part + 3))
        for c in range(NC):
            rows = slice(c * C, (c + 1) * C)
            cols = slice(part * 384, (part + 1) * 384)
            y = dot(h_ref[:C, c * M:(c + 1) * M], a_ref[:, cols])
            out_ref[rows, cols] = (acc_ref[rows, cols] + y).astype(BF16)

    def left(buf, count, sem):
        pltpu.make_async_copy(buf.at[pl.ds(0, count)], buf.at[pl.ds(0, count)], sem).wait()

    @pl.when(mine < OWN)
    def _():
        left(st_recv, 2 * OWN - 1, st_sem.at[0])

        @pl.when(my < 2)
        def _():
            left(pre_send, len(NEAR) + len(MIDWAY), pre_sem.at[0])

        @pl.when(my >= 2)
        def _():
            left(pre_send, len(NEAR), pre_sem.at[0])

    @pl.when(mine >= OWN)
    def _():
        left(st_recv, 2 * OWN, st_sem.at[0])
    for ch in range(CH):
        bulk(disp_send.at[ch], disp_ssem.at[ch]).wait()
        bulk(ret_send.at[ch], ret_ssem.at[ch]).wait()


def shards(queries, keys, values, norm_gain, expert_ids, w_in, w_out):
    hbm = pl.BlockSpec(memory_space=pltpu.HBM)
    vmem = pl.BlockSpec(memory_space=pltpu.VMEM)
    dma = pltpu.SemaphoreType.DMA
    return pl.pallas_call(
        body,
        out_shape=jax.ShapeDtypeStruct((T, D), BF16),
        in_specs=[hbm] * 7,
        out_specs=vmem,
        scratch_shapes=[
            pltpu.VMEM((D,), F32), pltpu.VMEM((1, T), jnp.int32),
            pltpu.VMEM((T, D), BF16), pltpu.VMEM((T, D), BF16), pltpu.VMEM((T, D), BF16),
            pltpu.VMEM((2, D, FF), BF16), pltpu.VMEM((2, FF, D), BF16),
            pltpu.VMEM((PAIRS, NC, 128, 128), F32), pltpu.VMEM((PAIRS, 128, 128), BF16),
            pltpu.VMEM((T, D), F32), pltpu.VMEM((T, D), BF16),
            pltpu.VMEM((OWN, 2, 8, 128), BF16), pltpu.VMEM((N, 2, 8, 128), BF16),
            pltpu.VMEM((N, 2, 8, 128), BF16), pltpu.VMEM((OWN, 2, 8, 128), BF16),
            pltpu.VMEM((T, 128), jnp.int32), pltpu.VMEM((M, D), F32), pltpu.VMEM((M, D), BF16),
            pltpu.VMEM((CH, N, 6, 8, 128), BF16), pltpu.VMEM((CH, N, 6, 8, 128), BF16),
            pltpu.VMEM((CH, N, 6, 8, 128), BF16), pltpu.VMEM((CH, N, 6, 8, 128), BF16),
            pltpu.VMEM((M, D), BF16), pltpu.VMEM((M, FF), BF16), pltpu.VMEM((T, D), F32),
            dma((5,)), dma((4,)), dma((8,)), dma((2,)), dma((2,)),
            dma((CH,)), dma((CH,)), dma((CH,)), dma((CH + 1,)),
        ],
        compiler_params=pltpu.CompilerParams(
            collective_id=0, has_side_effects=True, vmem_limit_bytes=52 * 2**20),
        name="block",
    )(queries, keys, values, pltpu.with_memory_space_constraint(norm_gain, pltpu.HBM),
      pltpu.with_memory_space_constraint(expert_ids.reshape(1, T), pltpu.HBM), w_in, w_out)


def solution(mesh):
    rows = P(("dp", "seq"), None)
    weights = P(("dp", "seq"), None, None)
    return jax.shard_map(
        shards, mesh=mesh, in_specs=(rows, rows, rows, P(), rows, weights, weights),
        out_specs=rows, check_vma=False)
```
